256 devices in a mesh: blk: 256 (over x, z, y, core).
Axes of the slice: x: 4, y: 4, z: 8, core: 2. Of those that a mesh axis runs over, the one named last changes fastest.
Arguments:
- traces: bfloat16 [32768, 144, 128], P('blk')
- bands: int32 [64], replicated, may hold values from 0 to 7, never falling along the last dimension, each value on 1 to 16 neighbouring positions
Outputs:
- cross_spectra: bfloat16 [32768, 2, 2, 64, 128], P('blk')
The draws below stay inside these ranges and needn't reach their ends.
Inputs may be any that keep to these rules, and one draw needn't show every extreme that they name: `bands`: band numbers never fall along the bins; every band holds 1 to 16 bins and one holds exactly 16.
All inputs are finite; a program needn't handle non-finite values.
Results may differ from the reference program's by a relative error of at most 0.024.
Values may be sent and summed in bfloat16 or wider, within the bound.
A program may use at most 128 MiB of HBM per device.

```python
import math
import jax
import jax.numpy as jnp
import numpy as np
from jax import lax

CH_DEV = 128
W = 144
L = 128
BINS = 64
HW = 16
RAM_HALF = 64
NBANDS = 8
BAND_MOST = 16
ROUNDS = 2
CHANNELS = 32768
N_BLK = 256


def draw_traces(key, part):
    keys = jax.random.split(jax.random.fold_in(key, 17), 4)
    top_scale = math.log(10.0)
    channel_scale = jnp.exp(jax.random.uniform(keys[0], (CHANNELS, 1, 1, 1), jnp.float32, 0.0, top_scale))
    envelope = jnp.exp(jax.random.uniform(keys[1], (CHANNELS, W, L // 16, 1), jnp.float32, math.log(0.3), math.log(3.0)))
    noise = jax.random.normal(keys[2], (CHANNELS, W, L // 16, 16), jnp.float32)
    common = 3.0 * jax.random.normal(keys[3], (1, W, L), jnp.float32)
    field = (channel_scale * envelope * noise).reshape(CHANNELS, W, L) + common
    return field.astype(jnp.bfloat16)


def profile(number_of, total, bound, slope):
    weights = [(1 << 20) // math.isqrt(grade ** slope) + 1 for grade in range(2, number_of + 1)]
    rest, counts = total - bound - (number_of - 1), [1] * (number_of - 1)
    while rest > 0:
        free = [i for i in range(number_of - 1) if counts[i] < bound]
        whole, budget = sum([weights[i] for i in free]), rest
        for i in free:
            addition = min(bound - counts[i], max(1, budget * weights[i] // whole), rest)
            counts[i] = counts[i] + addition
            rest = rest - addition
    return np.array([bound] + counts)


def ragged(key, number_of, total, limit, slope):
    if number_of == 2:
        one = jax.random.randint(key, (), max(1, total - limit), min(limit, total - 1) + 1)
        return jnp.stack([one, total - one])
    tallies = jnp.asarray(profile(number_of, total, limit, slope), jnp.int32)
    pairs = (number_of - 1) // 2
    source_of, sink = tallies[1:1 + 2 * pairs:2], tallies[2:2 + 2 * pairs:2]
    room = jnp.minimum(source_of - 1, limit - sink)
    passed = jax.random.randint(jax.random.fold_in(key, 1), (pairs,), 0, 1 << 20) % (room + 1)
    tallies = tallies.at[1:1 + 2 * pairs:2].set(source_of - passed).at[2:2 + 2 * pairs:2].set(sink + passed)
    return tallies[jax.random.permutation(jax.random.fold_in(key, 2), number_of)]


def setup_inputs(seed: int = 0) -> dict:
    arg_keys = jax.random.split(jax.random.key(seed), 3)
    traces = draw_traces(jax.random.fold_in(arg_keys[2], 71), 0)
    bands = jnp.searchsorted(jnp.cumsum(ragged(arg_keys[1], NBANDS, BINS, BAND_MOST, 0)), jnp.arange(BINS), side="right").astype(jnp.int32)
    return dict(traces=traces, bands=bands)


epsilon = 1e-05
floor_power = 0.25

def prepare(extended, first_channel, total_channels, bands, halo_width, ram_half):
    channel_count = extended.shape[0] - 2 * halo_width
    ext_rows = extended.shape[0]
    window_count = extended.shape[1]
    samples = extended.shape[2]
    bin_count = samples // 2
    inner = jnp.arange(channel_count, dtype=jnp.int32)
    outer = jnp.arange(ext_rows, dtype=jnp.int32)
    offset = outer[None, :] - inner[:, None]
    outer_position = first_channel - halo_width + outer
    inside = (outer_position >= 0) & (outer_position < total_channels)
    selector = ((offset >= 0) & (offset <= 2 * halo_width) & inside[None, :]).astype(jnp.float32)
    neighbour_count = lax.optimization_barrier(jnp.sum(selector, axis=1))
    neighbour_sum = jnp.einsum('ie,ewl->iwl', selector, extended.astype(jnp.float32))
    centred = extended[halo_width:halo_width + channel_count].astype(jnp.float32) - neighbour_sum / neighbour_count[:, None, None]
    balanced = centred.astype(jnp.bfloat16)
    magnitude = jnp.abs(balanced).astype(jnp.float32)
    sample_index = jnp.arange(samples, dtype=jnp.int32)
    ram_band = (jnp.abs(sample_index[:, None] - sample_index[None, :]) <= ram_half).astype(jnp.float32)
    ram_count = lax.optimization_barrier(jnp.sum(ram_band, axis=0))
    ram_sum = jnp.einsum('cwl,lm->cwm', magnitude, ram_band)
    envelope = ram_sum / ram_count + epsilon
    normalized = (balanced.astype(jnp.float32) / envelope).astype(jnp.bfloat16)
    frequency = jnp.arange(1, bin_count + 1, dtype=jnp.int32)
    phase_steps = frequency[:, None] * sample_index[None, :] % samples
    phase = 2.0 * math.pi / samples * phase_steps.astype(jnp.float32)
    dft_table = (jnp.concatenate([jnp.cos(phase), -jnp.sin(phase)], axis=0) / math.sqrt(samples)).astype(jnp.bfloat16)
    spectra = jnp.einsum('jl,cwl->jwc', dft_table.astype(jnp.float32), normalized.astype(jnp.float32))
    spectra = spectra.reshape(2, bin_count, window_count, channel_count)
    power_bins = spectra[0] * spectra[0] + spectra[1] * spectra[1]
    same_band = (bands[:, None] == bands[None, :]).astype(jnp.float32)
    band_matrix = same_band / lax.optimization_barrier(jnp.sum(same_band, axis=1, keepdims=True))
    band_mean = jnp.einsum('fg,gwc->fwc', band_matrix, power_bins, precision=lax.Precision.HIGHEST)
    whiten_scale = lax.rsqrt(jnp.maximum(band_mean, floor_power))
    return (spectra * whiten_scale[None]).astype(jnp.bfloat16)

def correlate(own_block, partner):
    flipped = jnp.stack([jnp.stack([partner[0], partner[1]]), jnp.stack([-partner[1], partner[0]])])
    window_count = own_block.shape[2]
    product = jnp.einsum('kfwc,okfwd->cofd', own_block.astype(jnp.float32), flipped.astype(jnp.float32))
    return (product / math.sqrt(window_count)).astype(jnp.bfloat16)

def reference(traces, bands):
    padded = jnp.pad(traces, ((HW, HW), (0, 0), (0, 0)))

    def one_block(block):
        start = (block * CH_DEV).astype(jnp.int32)
        extended = lax.dynamic_slice_in_dim(padded, start, CH_DEV + 2 * HW, 0)
        return prepare(extended, start, CHANNELS, bands, HW, RAM_HALF)
    whitened = lax.map(one_block, jnp.arange(N_BLK, dtype=jnp.int32))

    def tiles_of(block):
        own_block = whitened[block]
        results = []
        for round_index in range(ROUNDS):
            partner_index = ((block + round_index + 1) % N_BLK).astype(jnp.int32)
            results.append(correlate(own_block, whitened[partner_index]))
        return jnp.stack(results, axis=1)
    cross_tiles = lax.map(tiles_of, jnp.arange(N_BLK, dtype=jnp.int32))
    return cross_tiles.reshape(CHANNELS, ROUNDS, 2, BINS, CH_DEV)
```

```python
import math

import jax
import jax.numpy as jnp
from jax import lax
from jax.sharding import PartitionSpec as P

HW = 16
RAM_HALF = 64
ROUNDS = 2


epsilon = 1e-05
floor_power = 0.25


def with_halo(cells, sides, width):
    for axis, dim in sides:
        count = lax.axis_size(axis)
        ends = count - 1
        head = lax.slice_in_dim(cells, 0, width, axis=dim)
        tail = lax.slice_in_dim(cells, cells.shape[dim] - width, cells.shape[dim], axis=dim)
        cells = jnp.concatenate(
            [
                lax.ppermute(tail, axis, [(i, (i + 1) % count) for i in range(ends)]),
                cells,
                lax.ppermute(head, axis, [((i + 1) % count, i) for i in range(ends)]),
            ],
            axis=dim,
        )
    return cells


def shifted(shard, axis, by):
    count = lax.axis_size(axis)
    return lax.ppermute(shard, axis, [(i, (i + by) % count) for i in range(count)])


def prepare(extended, first_channel, total_channels, bands, halo_width, ram_half):
    channel_count = extended.shape[0] - 2 * halo_width
    ext_rows = extended.shape[0]
    window_count = extended.shape[1]
    samples = extended.shape[2]
    bin_count = samples // 2
    inner = jnp.arange(channel_count, dtype=jnp.int32)
    outer = jnp.arange(ext_rows, dtype=jnp.int32)
    offset = outer[None, :] - inner[:, None]
    outer_position = first_channel - halo_width + outer
    inside = (outer_position >= 0) & (outer_position < total_channels)
    selector = (offset >= 0) & (offset <= 2 * halo_width) & inside[None, :]
    neighbour_count = jnp.sum(selector.astype(jnp.float32), axis=1)
    neighbour_sum = jnp.einsum(
        "ie,ewl->iwl", selector.astype(jnp.bfloat16), extended, preferred_element_type=jnp.float32
    )
    centred = (
        extended[halo_width : halo_width + channel_count].astype(jnp.float32)
        - neighbour_sum / neighbour_count[:, None, None]
    )
    balanced = centred.astype(jnp.bfloat16)
    magnitude = jnp.abs(balanced)
    sample_index = jnp.arange(samples, dtype=jnp.int32)
    ram_band = jnp.abs(sample_index[:, None] - sample_index[None, :]) <= ram_half
    ram_count = jnp.sum(ram_band.astype(jnp.float32), axis=0)
    ram_sum = jnp.einsum(
        "cwl,lm->cwm", magnitude, ram_band.astype(jnp.bfloat16), preferred_element_type=jnp.float32
    )
    envelope = ram_sum / ram_count + epsilon
    normalized = (balanced.astype(jnp.float32) / envelope).astype(jnp.bfloat16)
    frequency = jnp.arange(1, bin_count + 1, dtype=jnp.int32)
    phase_steps = frequency[:, None] * sample_index[None, :] % samples
    phase = 2.0 * math.pi / samples * phase_steps.astype(jnp.float32)
    dft_table = (
        jnp.concatenate([jnp.cos(phase), -jnp.sin(phase)], axis=0) / math.sqrt(samples)
    ).astype(jnp.bfloat16)
    spectra = jnp.einsum("jl,cwl->jwc", dft_table, normalized, preferred_element_type=jnp.float32)
    spectra = spectra.reshape(2, bin_count, window_count, channel_count)
    power_bins = spectra[0] * spectra[0] + spectra[1] * spectra[1]
    same_band = (bands[:, None] == bands[None, :]).astype(jnp.float32)
    band_matrix = same_band / jnp.sum(same_band, axis=1, keepdims=True)
    band_mean = jnp.einsum("fg,gwc->fwc", band_matrix, power_bins, precision=lax.Precision.HIGHEST)
    whiten_scale = lax.rsqrt(jnp.maximum(band_mean, floor_power))
    return (spectra * whiten_scale[None]).astype(jnp.bfloat16)


def correlate(own_block, partner):
    flipped = jnp.stack([jnp.stack([partner[0], partner[1]]), jnp.stack([-partner[1], partner[0]])])
    window_count = own_block.shape[2]
    product = jnp.einsum("kfwc,okfwd->cofd", own_block, flipped, preferred_element_type=jnp.float32)
    return (product / math.sqrt(window_count)).astype(jnp.bfloat16)


def per_device(traces, bands):
    extended = with_halo(traces, (("blk", 0),), HW)
    channel_count = traces.shape[0]
    block_count = lax.axis_size("blk")
    first_channel = lax.axis_index("blk") * channel_count
    own_block = prepare(extended, first_channel, channel_count * block_count, bands, HW, RAM_HALF)
    second = shifted(own_block, "blk", -2)
    pairs_up = [(2 * i + 1, 2 * i) for i in range(block_count // 2)]
    pairs_down = [(2 * i, 2 * i + 1) for i in range(block_count // 2)]
    first = lax.ppermute(own_block, "blk", pairs_up) + lax.ppermute(second, "blk", pairs_down)
    results = [correlate(own_block, first), correlate(own_block, second)]
    return jnp.stack(results, axis=1)


def solution(mesh):
    placed = (P("blk", None, None), P())
    return jax.shard_map(
        per_device,
        mesh=mesh,
        in_specs=placed,
        out_specs=P("blk", None, None, None, None),
        check_vma=False,
    )
```

```python
import math

import jax
import jax.numpy as jnp
from jax import lax
from jax.sharding import PartitionSpec as P

HW = 16
RAM_HALF = 64
ROUNDS = 2


epsilon = 1e-05
floor_power = 0.25


def with_halo(cells, sides, width):
    for axis, dim in sides:
        count = lax.axis_size(axis)
        ends = count - 1
        head = lax.slice_in_dim(cells, 0, width, axis=dim)
        tail = lax.slice_in_dim(cells, cells.shape[dim] - width, cells.shape[dim], axis=dim)
        cells = jnp.concatenate(
            [
                lax.ppermute(tail, axis, [(i, (i + 1) % count) for i in range(ends)]),
                cells,
                lax.ppermute(head, axis, [((i + 1) % count, i) for i in range(ends)]),
            ],
            axis=dim,
        )
    return cells


def shifted(shard, axis, by):
    count = lax.axis_size(axis)
    return lax.ppermute(shard, axis, [(i, (i + by) % count) for i in range(count)])


def prepare(extended, first_channel, total_channels, bands, halo_width, ram_half):
    channel_count = extended.shape[0] - 2 * halo_width
    ext_rows = extended.shape[0]
    window_count = extended.shape[1]
    samples = extended.shape[2]
    bin_count = samples // 2
    inner = jnp.arange(channel_count, dtype=jnp.int32)
    outer = jnp.arange(ext_rows, dtype=jnp.int32)
    offset = outer[None, :] - inner[:, None]
    outer_position = first_channel - halo_width + outer
    inside = (outer_position >= 0) & (outer_position < total_channels)
    selector = (offset >= 0) & (offset <= 2 * halo_width) & inside[None, :]
    neighbour_count = jnp.sum(selector.astype(jnp.float32), axis=1)
    neighbour_sum = jnp.einsum(
        "ie,ewl->iwl", selector.astype(jnp.bfloat16), extended, preferred_element_type=jnp.float32
    )
    centred = (
        extended[halo_width : halo_width + channel_count].astype(jnp.float32)
        - neighbour_sum / neighbour_count[:, None, None]
    )
    balanced = centred.astype(jnp.bfloat16)
    magnitude = jnp.abs(balanced)
    sample_index = jnp.arange(samples, dtype=jnp.int32)
    ram_band = jnp.abs(sample_index[:, None] - sample_index[None, :]) <= ram_half
    ram_count = jnp.sum(ram_band.astype(jnp.float32), axis=0)
    ram_sum = jnp.einsum(
        "cwl,lm->cwm", magnitude, ram_band.astype(jnp.bfloat16), preferred_element_type=jnp.float32
    )
    envelope = ram_sum / ram_count + epsilon
    normalized = (balanced.astype(jnp.float32) / envelope).astype(jnp.bfloat16)
    frequency = jnp.arange(1, bin_count + 1, dtype=jnp.int32)
    phase_steps = frequency[:, None] * sample_index[None, :] % samples
    phase = 2.0 * math.pi / samples * phase_steps.astype(jnp.float32)
    dft_table = (
        jnp.concatenate([jnp.cos(phase), -jnp.sin(phase)], axis=0) / math.sqrt(samples)
    ).astype(jnp.bfloat16)
    spectra = jnp.einsum("jl,cwl->jwc", dft_table, normalized, preferred_element_type=jnp.float32)
    spectra = spectra.reshape(2, bin_count, window_count, channel_count)
    power_bins = spectra[0] * spectra[0] + spectra[1] * spectra[1]
    same_band = (bands[:, None] == bands[None, :]).astype(jnp.float32)
    band_matrix = same_band / jnp.sum(same_band, axis=1, keepdims=True)
    band_mean = jnp.einsum("fg,gwc->fwc", band_matrix, power_bins, precision=lax.Precision.HIGHEST)
    whiten_scale = lax.rsqrt(jnp.maximum(band_mean, floor_power))
    return (spectra * whiten_scale[None]).astype(jnp.bfloat16)


def correlate(own_block, partner):
    flipped = jnp.stack([jnp.stack([partner[0], partner[1]]), jnp.stack([-partner[1], partner[0]])])
    return jnp.einsum("kfwc,okfwd->cofd", own_block, flipped, preferred_element_type=jnp.float32)


def per_device(traces, bands, chunks=4):
    extended = with_halo(traces, (("blk", 0),), HW)
    channel_count = traces.shape[0]
    window_count = traces.shape[1]
    block_count = lax.axis_size("blk")
    first_channel = lax.axis_index("blk") * channel_count
    pairs_up = [(2 * i + 1, 2 * i) for i in range(block_count // 2)]
    pairs_down = [(2 * i, 2 * i + 1) for i in range(block_count // 2)]
    step = window_count // chunks
    totals = [None, None]
    for chunk in range(chunks):
        piece = extended[:, chunk * step : (chunk + 1) * step]
        own_block = prepare(piece, first_channel, channel_count * block_count, bands, HW, RAM_HALF)
        second = shifted(own_block, "blk", -2)
        first = lax.ppermute(own_block, "blk", pairs_up) + lax.ppermute(second, "blk", pairs_down)
        for r, partner in enumerate((first, second)):
            term = correlate(own_block, partner)
            totals[r] = term if totals[r] is None else totals[r] + term
    scale = 1.0 / math.sqrt(window_count)
    return jnp.stack([(t * scale).astype(jnp.bfloat16) for t in totals], axis=1)


def solution(mesh):
    placed = (P("blk", None, None), P())
    return jax.shard_map(
        per_device,
        mesh=mesh,
        in_specs=placed,
        out_specs=P("blk", None, None, None, None),
        check_vma=False,
    )
```

```python
import functools
import math

import jax
import jax.numpy as jnp
from jax import lax
from jax.experimental import pallas as pl
from jax.experimental.pallas import tpu as pltpu
from jax.sharding import PartitionSpec as P

MESH = pl.DeviceIdType.MESH

HW = 16
RAM_HALF = 64
ROUNDS = 2


epsilon = 1e-05
floor_power = 0.25


def with_halo(cells, sides, width):
    for axis, dim in sides:
        count = lax.axis_size(axis)
        ends = count - 1
        head = lax.slice_in_dim(cells, 0, width, axis=dim)
        tail = lax.slice_in_dim(cells, cells.shape[dim] - width, cells.shape[dim], axis=dim)
        cells = jnp.concatenate(
            [
                lax.ppermute(tail, axis, [(i, (i + 1) % count) for i in range(ends)]),
                cells,
                lax.ppermute(head, axis, [((i + 1) % count, i) for i in range(ends)]),
            ],
            axis=dim,
        )
    return cells


def shifted(shard, axis, by):
    count = lax.axis_size(axis)
    return lax.ppermute(shard, axis, [(i, (i + by) % count) for i in range(count)])


def prepare(extended, first_channel, total_channels, bands, halo_width, ram_half):
    channel_count = extended.shape[0] - 2 * halo_width
    ext_rows = extended.shape[0]
    window_count = extended.shape[1]
    samples = extended.shape[2]
    bin_count = samples // 2
    inner = jnp.arange(channel_count, dtype=jnp.int32)
    outer = jnp.arange(ext_rows, dtype=jnp.int32)
    offset = outer[None, :] - inner[:, None]
    outer_position = first_channel - halo_width + outer
    inside = (outer_position >= 0) & (outer_position < total_channels)
    selector = (offset >= 0) & (offset <= 2 * halo_width) & inside[None, :]
    neighbour_count = jnp.sum(selector.astype(jnp.float32), axis=1)
    neighbour_sum = jnp.einsum(
        "ie,ewl->iwl", selector.astype(jnp.bfloat16), extended, preferred_element_type=jnp.float32
    )
    centred = (
        extended[halo_width : halo_width + channel_count].astype(jnp.float32)
        - neighbour_sum / neighbour_count[:, None, None]
    )
    balanced = centred.astype(jnp.bfloat16)
    magnitude = jnp.abs(balanced)
    sample_index = jnp.arange(samples, dtype=jnp.int32)
    ram_band = jnp.abs(sample_index[:, None] - sample_index[None, :]) <= ram_half
    ram_count = jnp.sum(ram_band.astype(jnp.float32), axis=0)
    ram_sum = jnp.einsum(
        "cwl,lm->cwm", magnitude, ram_band.astype(jnp.bfloat16), preferred_element_type=jnp.float32
    )
    envelope = ram_sum / ram_count + epsilon
    normalized = (balanced.astype(jnp.float32) / envelope).astype(jnp.bfloat16)
    frequency = jnp.arange(1, bin_count + 1, dtype=jnp.int32)
    phase_steps = frequency[:, None] * sample_index[None, :] % samples
    phase = 2.0 * math.pi / samples * phase_steps.astype(jnp.float32)
    dft_table = (
        jnp.concatenate([jnp.cos(phase), -jnp.sin(phase)], axis=0) / math.sqrt(samples)
    ).astype(jnp.bfloat16)
    spectra = jnp.einsum("jl,cwl->jwc", dft_table, normalized, preferred_element_type=jnp.float32)
    spectra = spectra.reshape(2, bin_count, window_count, channel_count)
    power_bins = spectra[0] * spectra[0] + spectra[1] * spectra[1]
    same_band = (bands[:, None] == bands[None, :]).astype(jnp.float32)
    band_matrix = same_band / jnp.sum(same_band, axis=1, keepdims=True)
    band_mean = jnp.einsum("fg,gwc->fwc", band_matrix, power_bins, precision=lax.Precision.HIGHEST)
    whiten_scale = lax.rsqrt(jnp.maximum(band_mean, floor_power))
    return (spectra * whiten_scale[None]).astype(jnp.bfloat16)


def correlate_chunk(own, partner, out, r, rows, scale):
    real_rows, imag_rows = [], []
    for j in range(rows.size):
        f = rows.start + j
        x = own[:, f]
        y = partner[:, f]
        lhs = x.reshape(-1, x.shape[-1])
        real_rhs = y.reshape(-1, y.shape[-1])
        imag_rhs = jnp.concatenate([-y[1], y[0]], axis=0)
        dims = (((0,), (0,)), ((), ()))
        real = lax.dot_general(lhs, real_rhs, dims, preferred_element_type=jnp.float32)
        imag = lax.dot_general(lhs, imag_rhs, dims, preferred_element_type=jnp.float32)
        real_rows.append(real / scale)
        imag_rows.append(imag / scale)
    out[:, r, 0, rows, :] = jnp.stack(real_rows, axis=1).astype(out.dtype)
    out[:, r, 1, rows, :] = jnp.stack(imag_rows, axis=1).astype(out.dtype)


def exchange_kernel(n, chunks, scale, own, out, first, second, first_send, first_recv, second_send, second_recv):
    me = lax.axis_index("blk")
    core = lax.rem(me, 2)
    down = lax.rem(me + n - 2, n)
    up = lax.rem(me + 2, n)
    mate = me + 1 - 2 * core

    barrier = pltpu.get_barrier_semaphore()
    for peer in (down, up, mate):
        pl.semaphore_signal(barrier, inc=1, device_id=(peer,), device_id_type=MESH)
    pl.semaphore_wait(barrier, 3)

    size = own.shape[1] // chunks

    def part(i):
        return pl.ds(pl.multiple_of(i * size, size), size)

    def to_down(i):
        return pltpu.make_async_remote_copy(
            own.at[:, part(i)], second.at[:, part(i)], second_send.at[i], second_recv.at[i],
            device_id=(down,), device_id_type=MESH)

    def to_mate(src, i):
        return pltpu.make_async_remote_copy(
            src.at[:, part(i)], first.at[:, part(i)], first_send.at[i], first_recv.at[i],
            device_id=(mate,), device_id_type=MESH)

    @pl.loop(0, chunks)
    def _(i):
        to_down(i).start()

    @pl.when(core == 1)
    def _():
        @pl.loop(0, chunks)
        def _(i):
            to_mate(own, i).start()

    @pl.loop(0, chunks)
    def _(i):
        to_down(i).wait_recv()

        @pl.when(core == 0)
        def _():
            to_mate(second, i).start()

        correlate_chunk(own, second, out, 1, part(i), scale)
        to_mate(second, i).wait_recv()
        correlate_chunk(own, first, out, 0, part(i), scale)

    @pl.loop(0, chunks)
    def _(i):
        to_down(i).wait_send()
        to_mate(second, i).wait_send()


def exchange(own_block, chunks=4):
    n = lax.axis_size("blk")
    parts, bins, windows, channels = own_block.shape
    out_shape = jax.ShapeDtypeStruct((channels, ROUNDS, 2, bins, channels), jnp.bfloat16)
    return pl.pallas_call(
        functools.partial(exchange_kernel, n, chunks, math.sqrt(windows)),
        out_shape=out_shape,
        in_specs=[pl.BlockSpec(memory_space=pltpu.VMEM)],
        out_specs=pl.BlockSpec(memory_space=pltpu.VMEM),
        scratch_shapes=[
            pltpu.VMEM(own_block.shape, own_block.dtype),
            pltpu.VMEM(own_block.shape, own_block.dtype),
            pltpu.SemaphoreType.DMA((chunks,)),
            pltpu.SemaphoreType.DMA((chunks,)),
            pltpu.SemaphoreType.DMA((chunks,)),
            pltpu.SemaphoreType.DMA((chunks,)),
        ],
        compiler_params=pltpu.CompilerParams(collective_id=0, has_side_effects=True),
    )(own_block)


def per_device(traces, bands):
    extended = with_halo(traces, (("blk", 0),), HW)
    channel_count = traces.shape[0]
    block_count = lax.axis_size("blk")
    first_channel = lax.axis_index("blk") * channel_count
    own_block = prepare(extended, first_channel, channel_count * block_count, bands, HW, RAM_HALF)
    return exchange(own_block)


def solution(mesh):
    placed = (P("blk", None, None), P())
    return jax.shard_map(
        per_device,
        mesh=mesh,
        in_specs=placed,
        out_specs=P("blk", None, None, None, None),
        check_vma=False,
    )
```

```python
import functools
import math

import jax
import jax.numpy as jnp
from jax import lax
from jax.experimental import pallas as pl
from jax.experimental.pallas import tpu as pltpu
from jax.sharding import PartitionSpec as P

MESH = pl.DeviceIdType.MESH

HW = 16
RAM_HALF = 64
ROUNDS = 2


epsilon = 1e-05
floor_power = 0.25


def with_halo(cells, sides, width):
    for axis, dim in sides:
        count = lax.axis_size(axis)
        ends = count - 1
        head = lax.slice_in_dim(cells, 0, width, axis=dim)
        tail = lax.slice_in_dim(cells, cells.shape[dim] - width, cells.shape[dim], axis=dim)
        cells = jnp.concatenate(
            [
                lax.ppermute(tail, axis, [(i, (i + 1) % count) for i in range(ends)]),
                cells,
                lax.ppermute(head, axis, [((i + 1) % count, i) for i in range(ends)]),
            ],
            axis=dim,
        )
    return cells


def shifted(shard, axis, by):
    count = lax.axis_size(axis)
    return lax.ppermute(shard, axis, [(i, (i + by) % count) for i in range(count)])


def prepare(extended, first_channel, total_channels, bands, halo_width, ram_half):
    channel_count = extended.shape[0] - 2 * halo_width
    ext_rows = extended.shape[0]
    window_count = extended.shape[1]
    samples = extended.shape[2]
    bin_count = samples // 2
    inner = jnp.arange(channel_count, dtype=jnp.int32)
    outer = jnp.arange(ext_rows, dtype=jnp.int32)
    offset = outer[None, :] - inner[:, None]
    outer_position = first_channel - halo_width + outer
    inside = (outer_position >= 0) & (outer_position < total_channels)
    selector = (offset >= 0) & (offset <= 2 * halo_width) & inside[None, :]
    neighbour_count = jnp.sum(selector.astype(jnp.float32), axis=1)
    neighbour_sum = jnp.einsum(
        "ie,ewl->iwl", selector.astype(jnp.bfloat16), extended, preferred_element_type=jnp.float32
    )
    centred = (
        extended[halo_width : halo_width + channel_count].astype(jnp.float32)
        - neighbour_sum / neighbour_count[:, None, None]
    )
    balanced = centred.astype(jnp.bfloat16)
    magnitude = jnp.abs(balanced)
    sample_index = jnp.arange(samples, dtype=jnp.int32)
    ram_band = jnp.abs(sample_index[:, None] - sample_index[None, :]) <= ram_half
    ram_count = jnp.sum(ram_band.astype(jnp.float32), axis=0)
    ram_sum = jnp.einsum(
        "cwl,lm->cwm", magnitude, ram_band.astype(jnp.bfloat16), preferred_element_type=jnp.float32
    )
    envelope = ram_sum / ram_count + epsilon
    normalized = (balanced.astype(jnp.float32) / envelope).astype(jnp.bfloat16)
    frequency = jnp.arange(1, bin_count + 1, dtype=jnp.int32)
    phase_steps = frequency[:, None] * sample_index[None, :] % samples
    phase = 2.0 * math.pi / samples * phase_steps.astype(jnp.float32)
    dft_table = (
        jnp.concatenate([jnp.cos(phase), -jnp.sin(phase)], axis=0) / math.sqrt(samples)
    ).astype(jnp.bfloat16)
    spectra = jnp.einsum("jl,cwl->jwc", dft_table, normalized, preferred_element_type=jnp.float32)
    spectra = spectra.reshape(2, bin_count, window_count, channel_count)
    power_bins = spectra[0] * spectra[0] + spectra[1] * spectra[1]
    same_band = (bands[:, None] == bands[None, :]).astype(jnp.float32)
    band_matrix = same_band / jnp.sum(same_band, axis=1, keepdims=True)
    band_mean = jnp.einsum("fg,gwc->fwc", band_matrix, power_bins, precision=lax.Precision.HIGHEST)
    whiten_scale = lax.rsqrt(jnp.maximum(band_mean, floor_power))
    return (spectra * whiten_scale[None]).astype(jnp.bfloat16)


def correlate_chunk(own, partner, out, r, rows, scale):
    real_rows, imag_rows = [], []
    for j in range(rows.size):
        f = rows.start + j
        x = own[:, f]
        y = partner[:, f]
        lhs = x.reshape(-1, x.shape[-1])
        real_rhs = y.reshape(-1, y.shape[-1])
        imag_rhs = jnp.concatenate([-y[1], y[0]], axis=0)
        dims = (((0,), (0,)), ((), ()))
        real = lax.dot_general(lhs, real_rhs, dims, preferred_element_type=jnp.float32)
        imag = lax.dot_general(lhs, imag_rhs, dims, preferred_element_type=jnp.float32)
        real_rows.append(real / scale)
        imag_rows.append(imag / scale)
    out[:, r, 0, rows, :] = jnp.stack(real_rows, axis=1).astype(out.dtype)
    out[:, r, 1, rows, :] = jnp.stack(imag_rows, axis=1).astype(out.dtype)


def exchange_kernel(n, chunks, scale, own, out, first, second, first_send, first_recv, second_send, second_recv):
    me = lax.axis_index("blk")
    core = lax.rem(me, 2)
    down = lax.rem(me + n - 2, n)
    up = lax.rem(me + 2, n)
    mate = me + 1 - 2 * core

    barrier = pltpu.get_barrier_semaphore()
    for peer in (down, up, mate):
        pl.semaphore_signal(barrier, inc=1, device_id=(peer,), device_id_type=MESH)
    pl.semaphore_wait(barrier, 3)

    size = own.shape[1] // chunks

    def part(i):
        return pl.ds(pl.multiple_of(i * size, size), size)

    def to_down(i):
        return pltpu.make_async_remote_copy(
            own.at[:, part(i)], second.at[:, part(i)], second_send.at[i], second_recv.at[i],
            device_id=(down,), device_id_type=MESH)

    def to_mate(src, i):
        return pltpu.make_async_remote_copy(
            src.at[:, part(i)], first.at[:, part(i)], first_send.at[i], first_recv.at[i],
            device_id=(mate,), device_id_type=MESH)

    @pl.loop(0, chunks)
    def _(i):
        to_down(i).start()

    @pl.when(core == 1)
    def _():
        @pl.loop(0, chunks)
        def _(i):
            to_mate(own, i).start()

    @pl.loop(0, chunks)
    def _(i):
        to_down(i).wait_recv()

        @pl.when(core == 0)
        def _():
            to_mate(second, i).start()

        correlate_chunk(own, second, out, 1, part(i), scale)
        to_mate(second, i).wait_recv()
        correlate_chunk(own, first, out, 0, part(i), scale)

    @pl.loop(0, chunks)
    def _(i):
        to_down(i).wait_send()
        to_mate(second, i).wait_send()


def exchange(own_block, chunks=4):
    n = lax.axis_size("blk")
    parts, bins, windows, channels = own_block.shape
    out_shape = jax.ShapeDtypeStruct((channels, ROUNDS, 2, bins, channels), jnp.bfloat16)
    return pl.pallas_call(
        functools.partial(exchange_kernel, n, chunks, math.sqrt(windows)),
        out_shape=out_shape,
        in_specs=[pl.BlockSpec(memory_space=pltpu.VMEM)],
        out_specs=pl.BlockSpec(memory_space=pltpu.VMEM),
        scratch_shapes=[
            pltpu.VMEM(own_block.shape, own_block.dtype),
            pltpu.VMEM(own_block.shape, own_block.dtype),
            pltpu.SemaphoreType.DMA((chunks,)),
            pltpu.SemaphoreType.DMA((chunks,)),
            pltpu.SemaphoreType.DMA((chunks,)),
            pltpu.SemaphoreType.DMA((chunks,)),
        ],
        compiler_params=pltpu.CompilerParams(collective_id=0, has_side_effects=True),
    )(own_block)


def prepare_kernel(ext_ref, sel_ref, count_ref, ram_ref, ram_count_ref, table_ref, band_ref, out_ref):
    halo = (ext_ref.shape[0] - sel_ref.shape[0]) // 2
    channels = sel_ref.shape[0]
    bins = band_ref.shape[0]
    block = jnp.swapaxes(ext_ref[...].astype(jnp.float32), 0, 1)
    sel = sel_ref[...]
    count = count_ref[...]
    ram = ram_ref[...]
    ram_count = ram_count_ref[...]
    table = table_ref[...]
    band = band_ref[...]
    rows = []
    for w in range(block.shape[0]):
        x = block[w]
        neighbour_sum = jnp.dot(sel, x.astype(jnp.bfloat16), preferred_element_type=jnp.float32)
        balanced = (x[halo : halo + channels] - neighbour_sum / count).astype(jnp.bfloat16)
        ram_sum = jnp.dot(jnp.abs(balanced), ram, preferred_element_type=jnp.float32)
        envelope = ram_sum / ram_count + epsilon
        normalized = (balanced.astype(jnp.float32) / envelope).astype(jnp.bfloat16)
        spectra = lax.dot_general(
            table, normalized, (((1,), (1,)), ((), ())), preferred_element_type=jnp.float32
        )
        real, imag = spectra[:bins], spectra[bins:]
        power = real * real + imag * imag
        band_mean = jnp.dot(band, power, precision=lax.Precision.HIGHEST, preferred_element_type=jnp.float32)
        scale = lax.rsqrt(jnp.maximum(band_mean, floor_power))
        rows.append(jnp.concatenate([real * scale, imag * scale], axis=0))
    whitened = jnp.swapaxes(jnp.stack(rows, axis=0), 0, 1).astype(out_ref.dtype)
    out_ref[0] = whitened[:bins]
    out_ref[1] = whitened[bins:]


def prepare_fast(extended, first_channel, total_channels, bands, halo_width, ram_half, windows_per_step=16):
    channel_count = extended.shape[0] - 2 * halo_width
    ext_rows = extended.shape[0]
    window_count = extended.shape[1]
    samples = extended.shape[2]
    bin_count = samples // 2
    inner = jnp.arange(channel_count, dtype=jnp.int32)
    outer = jnp.arange(ext_rows, dtype=jnp.int32)
    offset = outer[None, :] - inner[:, None]
    outer_position = first_channel - halo_width + outer
    inside = (outer_position >= 0) & (outer_position < total_channels)
    selector = (offset >= 0) & (offset <= 2 * halo_width) & inside[None, :]
    neighbour_count = jnp.sum(selector.astype(jnp.float32), axis=1)[:, None]
    sample_index = jnp.arange(samples, dtype=jnp.int32)
    ram_band = jnp.abs(sample_index[:, None] - sample_index[None, :]) <= ram_half
    ram_count = jnp.sum(ram_band.astype(jnp.float32), axis=0)[None, :]
    frequency = jnp.arange(1, bin_count + 1, dtype=jnp.int32)
    phase_steps = frequency[:, None] * sample_index[None, :] % samples
    phase = 2.0 * math.pi / samples * phase_steps.astype(jnp.float32)
    dft_table = (
        jnp.concatenate([jnp.cos(phase), -jnp.sin(phase)], axis=0) / math.sqrt(samples)
    ).astype(jnp.bfloat16)
    same_band = (bands[:, None] == bands[None, :]).astype(jnp.float32)
    band_matrix = same_band / jnp.sum(same_band, axis=1, keepdims=True)
    step = windows_per_step
    whole = lambda i: (0, 0)
    return pl.pallas_call(
        prepare_kernel,
        out_shape=jax.ShapeDtypeStruct((2, bin_count, window_count, channel_count), jnp.bfloat16),
        grid=(window_count // step,),
        in_specs=[
            pl.BlockSpec((ext_rows, step, samples), lambda i: (0, i, 0)),
            pl.BlockSpec((channel_count, ext_rows), whole),
            pl.BlockSpec((channel_count, 1), whole),
            pl.BlockSpec((samples, samples), whole),
            pl.BlockSpec((1, samples), whole),
            pl.BlockSpec((samples, samples), whole),
            pl.BlockSpec((bin_count, bin_count), whole),
        ],
        out_specs=pl.BlockSpec((2, bin_count, step, channel_count), lambda i: (0, 0, i, 0)),
    )(
        extended,
        selector.astype(jnp.bfloat16),
        neighbour_count,
        ram_band.astype(jnp.bfloat16),
        ram_count,
        dft_table,
        band_matrix,
    )


def per_device(traces, bands):
    extended = with_halo(traces, (("blk", 0),), HW)
    channel_count = traces.shape[0]
    block_count = lax.axis_size("blk")
    first_channel = lax.axis_index("blk") * channel_count
    own_block = prepare_fast(extended, first_channel, channel_count * block_count, bands, HW, RAM_HALF)
    return exchange(own_block)


def solution(mesh):
    placed = (P("blk", None, None), P())
    return jax.shard_map(
        per_device,
        mesh=mesh,
        in_specs=placed,
        out_specs=P("blk", None, None, None, None),
        check_vma=False,
    )
```

```python
import functools
import math

import jax
import jax.numpy as jnp
from jax import lax
from jax.experimental import pallas as pl
from jax.experimental.pallas import tpu as pltpu
from jax.sharding import PartitionSpec as P

MESH = pl.DeviceIdType.MESH

HW = 16
RAM_HALF = 64
ROUNDS = 2


epsilon = 1e-05
floor_power = 0.25


def with_halo(cells, sides, width):
    for axis, dim in sides:
        count = lax.axis_size(axis)
        ends = count - 1
        head = lax.slice_in_dim(cells, 0, width, axis=dim)
        tail = lax.slice_in_dim(cells, cells.shape[dim] - width, cells.shape[dim], axis=dim)
        cells = jnp.concatenate(
            [
                lax.ppermute(tail, axis, [(i, (i + 1) % count) for i in range(ends)]),
                cells,
                lax.ppermute(head, axis, [((i + 1) % count, i) for i in range(ends)]),
            ],
            axis=dim,
        )
    return cells


def shifted(shard, axis, by):
    count = lax.axis_size(axis)
    return lax.ppermute(shard, axis, [(i, (i + by) % count) for i in range(count)])


def prepare(extended, first_channel, total_channels, bands, halo_width, ram_half):
    channel_count = extended.shape[0] - 2 * halo_width
    ext_rows = extended.shape[0]
    window_count = extended.shape[1]
    samples = extended.shape[2]
    bin_count = samples // 2
    inner = jnp.arange(channel_count, dtype=jnp.int32)
    outer = jnp.arange(ext_rows, dtype=jnp.int32)
    offset = outer[None, :] - inner[:, None]
    outer_position = first_channel - halo_width + outer
    inside = (outer_position >= 0) & (outer_position < total_channels)
    selector = (offset >= 0) & (offset <= 2 * halo_width) & inside[None, :]
    neighbour_count = jnp.sum(selector.astype(jnp.float32), axis=1)
    neighbour_sum = jnp.einsum(
        "ie,ewl->iwl", selector.astype(jnp.bfloat16), extended, preferred_element_type=jnp.float32
    )
    centred = (
        extended[halo_width : halo_width + channel_count].astype(jnp.float32)
        - neighbour_sum / neighbour_count[:, None, None]
    )
    balanced = centred.astype(jnp.bfloat16)
    magnitude = jnp.abs(balanced)
    sample_index = jnp.arange(samples, dtype=jnp.int32)
    ram_band = jnp.abs(sample_index[:, None] - sample_index[None, :]) <= ram_half
    ram_count = jnp.sum(ram_band.astype(jnp.float32), axis=0)
    ram_sum = jnp.einsum(
        "cwl,lm->cwm", magnitude, ram_band.astype(jnp.bfloat16), preferred_element_type=jnp.float32
    )
    envelope = ram_sum / ram_count + epsilon
    normalized = (balanced.astype(jnp.float32) / envelope).astype(jnp.bfloat16)
    frequency = jnp.arange(1, bin_count + 1, dtype=jnp.int32)
    phase_steps = frequency[:, None] * sample_index[None, :] % samples
    phase = 2.0 * math.pi / samples * phase_steps.astype(jnp.float32)
    dft_table = (
        jnp.concatenate([jnp.cos(phase), -jnp.sin(phase)], axis=0) / math.sqrt(samples)
    ).astype(jnp.bfloat16)
    spectra = jnp.einsum("jl,cwl->jwc", dft_table, normalized, preferred_element_type=jnp.float32)
    spectra = spectra.reshape(2, bin_count, window_count, channel_count)
    power_bins = spectra[0] * spectra[0] + spectra[1] * spectra[1]
    same_band = (bands[:, None] == bands[None, :]).astype(jnp.float32)
    band_matrix = same_band / jnp.sum(same_band, axis=1, keepdims=True)
    band_mean = jnp.einsum("fg,gwc->fwc", band_matrix, power_bins, precision=lax.Precision.HIGHEST)
    whiten_scale = lax.rsqrt(jnp.maximum(band_mean, floor_power))
    return (spectra * whiten_scale[None]).astype(jnp.bfloat16)


def whiten_block(block, sel, count, ram, ram_count, table, band):
    halo = (block.shape[0] - sel.shape[0]) // 2
    channels = sel.shape[0]
    bins = band.shape[0]
    block = jnp.swapaxes(block.astype(jnp.float32), 0, 1)
    rows = []
    for w in range(block.shape[0]):
        x = block[w]
        neighbour_sum = jnp.dot(sel, x.astype(jnp.bfloat16), preferred_element_type=jnp.float32)
        balanced = (x[halo : halo + channels] - neighbour_sum / count).astype(jnp.bfloat16)
        ram_sum = jnp.dot(jnp.abs(balanced), ram, preferred_element_type=jnp.float32)
        envelope = ram_sum / ram_count + epsilon
        normalized = (balanced.astype(jnp.float32) / envelope).astype(jnp.bfloat16)
        spectra = lax.dot_general(
            table, normalized, (((1,), (1,)), ((), ())), preferred_element_type=jnp.float32
        )
        real, imag = spectra[:bins], spectra[bins:]
        power = real * real + imag * imag
        band_mean = jnp.dot(band, power, precision=lax.Precision.HIGHEST, preferred_element_type=jnp.float32)
        scale = lax.rsqrt(jnp.maximum(band_mean, floor_power))
        rows.append(jnp.concatenate([real * scale, imag * scale], axis=0))
    whitened = jnp.swapaxes(jnp.stack(rows, axis=0), 0, 1)
    return whitened.reshape(2, bins, whitened.shape[1], channels)


def prepare_kernel(ext_ref, sel_ref, count_ref, ram_ref, ram_count_ref, table_ref, band_ref, out_ref):
    consts = [r[...] for r in (sel_ref, count_ref, ram_ref, ram_count_ref, table_ref, band_ref)]
    out_ref[...] = whiten_block(ext_ref[...], *consts).astype(out_ref.dtype)


def constants(first_channel, total_channels, bands, channel_count, halo_width, samples, ram_half):
    ext_rows = channel_count + 2 * halo_width
    bin_count = samples // 2
    inner = jnp.arange(channel_count, dtype=jnp.int32)
    outer = jnp.arange(ext_rows, dtype=jnp.int32)
    offset = outer[None, :] - inner[:, None]
    outer_position = first_channel - halo_width + outer
    inside = (outer_position >= 0) & (outer_position < total_channels)
    selector = (offset >= 0) & (offset <= 2 * halo_width) & inside[None, :]
    neighbour_count = jnp.sum(selector.astype(jnp.float32), axis=1)[:, None]
    sample_index = jnp.arange(samples, dtype=jnp.int32)
    ram_band = jnp.abs(sample_index[:, None] - sample_index[None, :]) <= ram_half
    ram_count = jnp.sum(ram_band.astype(jnp.float32), axis=0)[None, :]
    frequency = jnp.arange(1, bin_count + 1, dtype=jnp.int32)
    phase_steps = frequency[:, None] * sample_index[None, :] % samples
    phase = 2.0 * math.pi / samples * phase_steps.astype(jnp.float32)
    dft_table = (
        jnp.concatenate([jnp.cos(phase), -jnp.sin(phase)], axis=0) / math.sqrt(samples)
    ).astype(jnp.bfloat16)
    same_band = (bands[:, None] == bands[None, :]).astype(jnp.float32)
    band_matrix = same_band / jnp.sum(same_band, axis=1, keepdims=True)
    return [
        selector.astype(jnp.bfloat16),
        neighbour_count,
        ram_band.astype(jnp.bfloat16),
        ram_count,
        dft_table,
        band_matrix,
    ]


def prepare_fast(extended, consts, windows, step=16):
    ext_rows, _, samples = extended.shape
    channel_count = consts[0].shape[0]
    bin_count = samples // 2
    whole = lambda i: (0, 0)
    return pl.pallas_call(
        prepare_kernel,
        out_shape=jax.ShapeDtypeStruct((2, bin_count, windows, channel_count), jnp.bfloat16),
        grid=(windows // step,),
        in_specs=[pl.BlockSpec((ext_rows, step, samples), lambda i: (0, i, 0))]
        + [pl.BlockSpec(c.shape, whole) for c in consts],
        out_specs=pl.BlockSpec((2, bin_count, step, channel_count), lambda i: (0, 0, i, 0)),
    )(extended, *consts)


def correlate_chunk(owns, partners, out, r, rows, scale):
    dims = (((0,), (0,)), ((), ()))
    real_rows, imag_rows = [], []
    for j in range(rows.size):
        f = rows.start + j
        real, imag = 0.0, 0.0
        for own, partner in zip(owns, partners):
            x = own[:, f]
            y = partner[:, f]
            lhs = x.reshape(-1, x.shape[-1])
            real_rhs = y.reshape(-1, y.shape[-1])
            imag_rhs = jnp.concatenate([-y[1], y[0]], axis=0)
            real = real + lax.dot_general(lhs, real_rhs, dims, preferred_element_type=jnp.float32)
            imag = imag + lax.dot_general(lhs, imag_rhs, dims, preferred_element_type=jnp.float32)
        real_rows.append(real / scale)
        imag_rows.append(imag / scale)
    out[:, r, 0, rows, :] = jnp.stack(real_rows, axis=1).astype(out.dtype)
    out[:, r, 1, rows, :] = jnp.stack(imag_rows, axis=1).astype(out.dtype)


def exchange_kernel(n, chunks, scale, step, early, ext, sel, count, ram, ram_count, table, band,
                    out, late, first, second, first_send, first_recv, second_send, second_recv):
    me = lax.axis_index("blk")
    core = lax.rem(me, 2)
    down = lax.rem(me + n - 2, n)
    up = lax.rem(me + 2, n)
    mate = me + 1 - 2 * core

    barrier = pltpu.get_barrier_semaphore()
    for peer in (down, up, mate):
        pl.semaphore_signal(barrier, inc=1, device_id=(peer,), device_id_type=MESH)
    pl.semaphore_wait(barrier, 3)

    size = early.shape[1] // chunks
    owns = (early, late)

    def part(i):
        return pl.ds(pl.multiple_of(i * size, size), size)

    def to_down(p, i):
        return pltpu.make_async_remote_copy(
            owns[p].at[:, part(i)], second[p].at[:, part(i)], second_send.at[p, i], second_recv.at[p, i],
            device_id=(down,), device_id_type=MESH)

    def to_mate(src, p, i):
        return pltpu.make_async_remote_copy(
            src.at[:, part(i)], first[p].at[:, part(i)], first_send.at[p, i], first_recv.at[p, i],
            device_id=(mate,), device_id_type=MESH)

    def send_part(p):
        @pl.loop(0, chunks)
        def _(i):
            to_down(p, i).start()

        @pl.when(core == 1)
        def _():
            @pl.loop(0, chunks)
            def _(i):
                to_mate(owns[p], p, i).start()

    send_part(0)

    consts = [r[...] for r in (sel, count, ram, ram_count, table, band)]

    @pl.loop(0, ext.shape[1] // step)
    def _(b):
        windows = pl.ds(pl.multiple_of(b * step, step), step)
        late[:, :, windows, :] = whiten_block(ext[:, windows, :], *consts).astype(late.dtype)

    send_part(1)

    @pl.loop(0, chunks)
    def _(i):
        for p in range(2):
            to_down(p, i).wait_recv()

            @pl.when(core == 0)
            def _():
                to_mate(second[p], p, i).start()

        correlate_chunk(owns, second, out, 1, part(i), scale)
        for p in range(2):
            to_mate(second[p], p, i).wait_recv()
        correlate_chunk(owns, first, out, 0, part(i), scale)

    @pl.loop(0, chunks)
    def _(i):
        for p in range(2):
            to_down(p, i).wait_send()
            to_mate(second[p], p, i).wait_send()


def per_device(traces, bands, chunks=4, early_windows=64):
    extended = with_halo(traces, (("blk", 0),), HW)
    channel_count, window_count, samples = traces.shape
    n = lax.axis_size("blk")
    first_channel = lax.axis_index("blk") * channel_count
    consts = constants(first_channel, channel_count * n, bands, channel_count, HW, samples, RAM_HALF)
    early = prepare_fast(extended, consts, early_windows)
    rest = extended[:, early_windows:]
    bins = samples // 2
    late_shape = (2, bins, window_count - early_windows, channel_count)
    vmem = pl.BlockSpec(memory_space=pltpu.VMEM)
    return pl.pallas_call(
        functools.partial(exchange_kernel, n, chunks, math.sqrt(window_count), 16),
        out_shape=jax.ShapeDtypeStruct((channel_count, ROUNDS, 2, bins, channel_count), jnp.bfloat16),
        in_specs=[vmem] * 8,
        out_specs=vmem,
        scratch_shapes=[
            pltpu.VMEM(late_shape, jnp.bfloat16),
            [pltpu.VMEM(early.shape, jnp.bfloat16), pltpu.VMEM(late_shape, jnp.bfloat16)],
            [pltpu.VMEM(early.shape, jnp.bfloat16), pltpu.VMEM(late_shape, jnp.bfloat16)],
            pltpu.SemaphoreType.DMA((2, chunks)),
            pltpu.SemaphoreType.DMA((2, chunks)),
            pltpu.SemaphoreType.DMA((2, chunks)),
            pltpu.SemaphoreType.DMA((2, chunks)),
        ],
        compiler_params=pltpu.CompilerParams(
            collective_id=0, has_side_effects=True, vmem_limit_bytes=60 * 1024 * 1024
        ),
    )(early, rest, *consts)


def solution(mesh):
    placed = (P("blk", None, None), P())
    return jax.shard_map(
        per_device,
        mesh=mesh,
        in_specs=placed,
        out_specs=P("blk", None, None, None, None),
        check_vma=False,
    )
```

```python
import functools
import math

import jax
import jax.numpy as jnp
from jax import lax
from jax.experimental import pallas as pl
from jax.experimental.pallas import tpu as pltpu
from jax.sharding import PartitionSpec as P

MESH = pl.DeviceIdType.MESH

HW = 16
RAM_HALF = 64
ROUNDS = 2


epsilon = 1e-05
floor_power = 0.25


def with_halo(cells, sides, width):
    for axis, dim in sides:
        count = lax.axis_size(axis)
        ends = count - 1
        head = lax.slice_in_dim(cells, 0, width, axis=dim)
        tail = lax.slice_in_dim(cells, cells.shape[dim] - width, cells.shape[dim], axis=dim)
        cells = jnp.concatenate(
            [
                lax.ppermute(tail, axis, [(i, (i + 1) % count) for i in range(ends)]),
                cells,
                lax.ppermute(head, axis, [((i + 1) % count, i) for i in range(ends)]),
            ],
            axis=dim,
        )
    return cells


def shifted(shard, axis, by):
    count = lax.axis_size(axis)
    return lax.ppermute(shard, axis, [(i, (i + by) % count) for i in range(count)])


def prepare(extended, first_channel, total_channels, bands, halo_width, ram_half):
    channel_count = extended.shape[0] - 2 * halo_width
    ext_rows = extended.shape[0]
    window_count = extended.shape[1]
    samples = extended.shape[2]
    bin_count = samples // 2
    inner = jnp.arange(channel_count, dtype=jnp.int32)
    outer = jnp.arange(ext_rows, dtype=jnp.int32)
    offset = outer[None, :] - inner[:, None]
    outer_position = first_channel - halo_width + outer
    inside = (outer_position >= 0) & (outer_position < total_channels)
    selector = (offset >= 0) & (offset <= 2 * halo_width) & inside[None, :]
    neighbour_count = jnp.sum(selector.astype(jnp.float32), axis=1)
    neighbour_sum = jnp.einsum(
        "ie,ewl->iwl", selector.astype(jnp.bfloat16), extended, preferred_element_type=jnp.float32
    )
    centred = (
        extended[halo_width : halo_width + channel_count].astype(jnp.float32)
        - neighbour_sum / neighbour_count[:, None, None]
    )
    balanced = centred.astype(jnp.bfloat16)
    magnitude = jnp.abs(balanced)
    sample_index = jnp.arange(samples, dtype=jnp.int32)
    ram_band = jnp.abs(sample_index[:, None] - sample_index[None, :]) <= ram_half
    ram_count = jnp.sum(ram_band.astype(jnp.float32), axis=0)
    ram_sum = jnp.einsum(
        "cwl,lm->cwm", magnitude, ram_band.astype(jnp.bfloat16), preferred_element_type=jnp.float32
    )
    envelope = ram_sum / ram_count + epsilon
    normalized = (balanced.astype(jnp.float32) / envelope).astype(jnp.bfloat16)
    frequency = jnp.arange(1, bin_count + 1, dtype=jnp.int32)
    phase_steps = frequency[:, None] * sample_index[None, :] % samples
    phase = 2.0 * math.pi / samples * phase_steps.astype(jnp.float32)
    dft_table = (
        jnp.concatenate([jnp.cos(phase), -jnp.sin(phase)], axis=0) / math.sqrt(samples)
    ).astype(jnp.bfloat16)
    spectra = jnp.einsum("jl,cwl->jwc", dft_table, normalized, preferred_element_type=jnp.float32)
    spectra = spectra.reshape(2, bin_count, window_count, channel_count)
    power_bins = spectra[0] * spectra[0] + spectra[1] * spectra[1]
    same_band = (bands[:, None] == bands[None, :]).astype(jnp.float32)
    band_matrix = same_band / jnp.sum(same_band, axis=1, keepdims=True)
    band_mean = jnp.einsum("fg,gwc->fwc", band_matrix, power_bins, precision=lax.Precision.HIGHEST)
    whiten_scale = lax.rsqrt(jnp.maximum(band_mean, floor_power))
    return (spectra * whiten_scale[None]).astype(jnp.bfloat16)


def whiten_block(block, sel, count, ram, ram_count, table, band):
    halo = (block.shape[0] - sel.shape[0]) // 2
    channels = sel.shape[0]
    bins = band.shape[0]
    block = jnp.swapaxes(block.astype(jnp.float32), 0, 1)
    rows = []
    for w in range(block.shape[0]):
        x = block[w]
        neighbour_sum = jnp.dot(sel, x.astype(jnp.bfloat16), preferred_element_type=jnp.float32)
        balanced = (x[halo : halo + channels] - neighbour_sum / count).astype(jnp.bfloat16)
        ram_sum = jnp.dot(jnp.abs(balanced), ram, preferred_element_type=jnp.float32)
        envelope = ram_sum / ram_count + epsilon
        normalized = (balanced.astype(jnp.float32) / envelope).astype(jnp.bfloat16)
        spectra = lax.dot_general(
            table, normalized, (((1,), (1,)), ((), ())), preferred_element_type=jnp.float32
        )
        real, imag = spectra[:bins], spectra[bins:]
        power = real * real + imag * imag
        band_mean = jnp.dot(band, power, precision=lax.Precision.HIGHEST, preferred_element_type=jnp.float32)
        scale = lax.rsqrt(jnp.maximum(band_mean, floor_power))
        rows.append(jnp.concatenate([real * scale, imag * scale], axis=0))
    whitened = jnp.swapaxes(jnp.stack(rows, axis=0), 0, 1)
    return whitened.reshape(2, bins, whitened.shape[1], channels)


def prepare_kernel(ext_ref, sel_ref, count_ref, ram_ref, ram_count_ref, table_ref, band_ref, out_ref):
    consts = [r[...] for r in (sel_ref, count_ref, ram_ref, ram_count_ref, table_ref, band_ref)]
    out_ref[...] = whiten_block(ext_ref[...], *consts).astype(out_ref.dtype)


def constants(first_channel, total_channels, bands, channel_count, halo_width, samples, ram_half):
    ext_rows = channel_count + 2 * halo_width
    bin_count = samples // 2
    inner = jnp.arange(channel_count, dtype=jnp.int32)
    outer = jnp.arange(ext_rows, dtype=jnp.int32)
    offset = outer[None, :] - inner[:, None]
    outer_position = first_channel - halo_width + outer
    inside = (outer_position >= 0) & (outer_position < total_channels)
    selector = (offset >= 0) & (offset <= 2 * halo_width) & inside[None, :]
    neighbour_count = jnp.sum(selector.astype(jnp.float32), axis=1)[:, None]
    sample_index = jnp.arange(samples, dtype=jnp.int32)
    ram_band = jnp.abs(sample_index[:, None] - sample_index[None, :]) <= ram_half
    ram_count = jnp.sum(ram_band.astype(jnp.float32), axis=0)[None, :]
    frequency = jnp.arange(1, bin_count + 1, dtype=jnp.int32)
    phase_steps = frequency[:, None] * sample_index[None, :] % samples
    phase = 2.0 * math.pi / samples * phase_steps.astype(jnp.float32)
    dft_table = (
        jnp.concatenate([jnp.cos(phase), -jnp.sin(phase)], axis=0) / math.sqrt(samples)
    ).astype(jnp.bfloat16)
    same_band = (bands[:, None] == bands[None, :]).astype(jnp.float32)
    band_matrix = same_band / jnp.sum(same_band, axis=1, keepdims=True)
    return [
        selector.astype(jnp.bfloat16),
        neighbour_count,
        ram_band.astype(jnp.bfloat16),
        ram_count,
        dft_table,
        band_matrix,
    ]


def prepare_fast(extended, consts, windows, step=16):
    ext_rows, _, samples = extended.shape
    channel_count = consts[0].shape[0]
    bin_count = samples // 2
    whole = lambda i: (0, 0)
    return pl.pallas_call(
        prepare_kernel,
        out_shape=jax.ShapeDtypeStruct((2, bin_count, windows, channel_count), jnp.bfloat16),
        grid=(windows // step,),
        in_specs=[pl.BlockSpec((ext_rows, step, samples), lambda i: (0, i, 0))]
        + [pl.BlockSpec(c.shape, whole) for c in consts],
        out_specs=pl.BlockSpec((2, bin_count, step, channel_count), lambda i: (0, 0, i, 0)),
    )(extended, *consts)


def correlate_chunk(owns, partners, out, r, rows, scale):
    dims = (((0,), (0,)), ((), ()))
    real_rows, imag_rows = [], []
    for j in range(rows.size):
        f = rows.start + j
        real, imag = 0.0, 0.0
        for own, partner in zip(owns, partners):
            x = own[:, f]
            y = partner[:, f]
            lhs = x.reshape(-1, x.shape[-1])
            real_rhs = y.reshape(-1, y.shape[-1])
            imag_rhs = jnp.concatenate([-y[1], y[0]], axis=0)
            rhs = jnp.concatenate([real_rhs, imag_rhs], axis=1)
            both = lax.dot_general(lhs, rhs, dims, preferred_element_type=jnp.float32)
            real = real + both[:, : y.shape[-1]]
            imag = imag + both[:, y.shape[-1] :]
        real_rows.append(real / scale)
        imag_rows.append(imag / scale)
    out[:, r, 0, rows, :] = jnp.stack(real_rows, axis=1).astype(out.dtype)
    out[:, r, 1, rows, :] = jnp.stack(imag_rows, axis=1).astype(out.dtype)


def exchange_kernel(n, chunks, scale, step, early, ext, sel, count, ram, ram_count, table, band,
                    out, late, first, second, first_send, first_recv, second_send, second_recv):
    me = lax.axis_index("blk")
    core = lax.rem(me, 2)
    down = lax.rem(me + n - 2, n)
    up = lax.rem(me + 2, n)
    mate = me + 1 - 2 * core

    barrier = pltpu.get_barrier_semaphore()
    for peer in (down, up, mate):
        pl.semaphore_signal(barrier, inc=1, device_id=(peer,), device_id_type=MESH)
    pl.semaphore_wait(barrier, 3)

    size = early.shape[1] // chunks
    owns = (early, late)

    def part(i):
        return pl.ds(pl.multiple_of(i * size, size), size)

    def to_down(p, i):
        return pltpu.make_async_remote_copy(
            owns[p].at[:, part(i)], second[p].at[:, part(i)], second_send.at[p, i], second_recv.at[p, i],
            device_id=(down,), device_id_type=MESH)

    def to_mate(src, p, i):
        return pltpu.make_async_remote_copy(
            src.at[:, part(i)], first[p].at[:, part(i)], first_send.at[p, i], first_recv.at[p, i],
            device_id=(mate,), device_id_type=MESH)

    def send_part(p):
        @pl.loop(0, chunks)
        def _(i):
            to_down(p, i).start()

        @pl.when(core == 1)
        def _():
            @pl.loop(0, chunks)
            def _(i):
                to_mate(owns[p], p, i).start()

    send_part(0)

    consts = [r[...] for r in (sel, count, ram, ram_count, table, band)]

    @pl.loop(0, ext.shape[1] // step)
    def _(b):
        windows = pl.ds(pl.multiple_of(b * step, step), step)
        late[:, :, windows, :] = whiten_block(ext[:, windows, :], *consts).astype(late.dtype)

    send_part(1)

    @pl.loop(0, chunks)
    def _(i):
        for p in range(2):
            to_down(p, i).wait_recv()

            @pl.when(core == 0)
            def _():
                to_mate(second[p], p, i).start()

        correlate_chunk(owns, second, out, 1, part(i), scale)
        for p in range(2):
            to_mate(second[p], p, i).wait_recv()
        correlate_chunk(owns, first, out, 0, part(i), scale)

    @pl.loop(0, chunks)
    def _(i):
        for p in range(2):
            to_down(p, i).wait_send()
            to_mate(second[p], p, i).wait_send()


def per_device(traces, bands, chunks=4, early_windows=64):
    extended = with_halo(traces, (("blk", 0),), HW)
    channel_count, window_count, samples = traces.shape
    n = lax.axis_size("blk")
    first_channel = lax.axis_index("blk") * channel_count
    consts = constants(first_channel, channel_count * n, bands, channel_count, HW, samples, RAM_HALF)
    early = prepare_fast(extended, consts, early_windows)
    rest = extended[:, early_windows:]
    bins = samples // 2
    late_shape = (2, bins, window_count - early_windows, channel_count)
    vmem = pl.BlockSpec(memory_space=pltpu.VMEM)
    return pl.pallas_call(
        functools.partial(exchange_kernel, n, chunks, math.sqrt(window_count), 16),
        out_shape=jax.ShapeDtypeStruct((channel_count, ROUNDS, 2, bins, channel_count), jnp.bfloat16),
        in_specs=[vmem] * 8,
        out_specs=vmem,
        scratch_shapes=[
            pltpu.VMEM(late_shape, jnp.bfloat16),
            [pltpu.VMEM(early.shape, jnp.bfloat16), pltpu.VMEM(late_shape, jnp.bfloat16)],
            [pltpu.VMEM(early.shape, jnp.bfloat16), pltpu.VMEM(late_shape, jnp.bfloat16)],
            pltpu.SemaphoreType.DMA((2, chunks)),
            pltpu.SemaphoreType.DMA((2, chunks)),
            pltpu.SemaphoreType.DMA((2, chunks)),
            pltpu.SemaphoreType.DMA((2, chunks)),
        ],
        compiler_params=pltpu.CompilerParams(
            collective_id=0, has_side_effects=True, vmem_limit_bytes=60 * 1024 * 1024
        ),
    )(early, rest, *consts)


def solution(mesh):
    placed = (P("blk", None, None), P())
    return jax.shard_map(
        per_device,
        mesh=mesh,
        in_specs=placed,
        out_specs=P("blk", None, None, None, None),
        check_vma=False,
    )
```

```python
import functools
import math

import jax
import jax.numpy as jnp
from jax import lax
from jax.experimental import pallas as pl
from jax.experimental.pallas import tpu as pltpu
from jax.sharding import PartitionSpec as P

MESH = pl.DeviceIdType.MESH

HW = 16
RAM_HALF = 64
ROUNDS = 2


epsilon = 1e-05
floor_power = 0.25


def with_halo(cells, sides, width):
    for axis, dim in sides:
        count = lax.axis_size(axis)
        ends = count - 1
        head = lax.slice_in_dim(cells, 0, width, axis=dim)
        tail = lax.slice_in_dim(cells, cells.shape[dim] - width, cells.shape[dim], axis=dim)
        cells = jnp.concatenate(
            [
                lax.ppermute(tail, axis, [(i, (i + 1) % count) for i in range(ends)]),
                cells,
                lax.ppermute(head, axis, [((i + 1) % count, i) for i in range(ends)]),
            ],
            axis=dim,
        )
    return cells


def shifted(shard, axis, by):
    count = lax.axis_size(axis)
    return lax.ppermute(shard, axis, [(i, (i + by) % count) for i in range(count)])


def prepare(extended, first_channel, total_channels, bands, halo_width, ram_half):
    channel_count = extended.shape[0] - 2 * halo_width
    ext_rows = extended.shape[0]
    window_count = extended.shape[1]
    samples = extended.shape[2]
    bin_count = samples // 2
    inner = jnp.arange(channel_count, dtype=jnp.int32)
    outer = jnp.arange(ext_rows, dtype=jnp.int32)
    offset = outer[None, :] - inner[:, None]
    outer_position = first_channel - halo_width + outer
    inside = (outer_position >= 0) & (outer_position < total_channels)
    selector = (offset >= 0) & (offset <= 2 * halo_width) & inside[None, :]
    neighbour_count = jnp.sum(selector.astype(jnp.float32), axis=1)
    neighbour_sum = jnp.einsum(
        "ie,ewl->iwl", selector.astype(jnp.bfloat16), extended, preferred_element_type=jnp.float32
    )
    centred = (
        extended[halo_width : halo_width + channel_count].astype(jnp.float32)
        - neighbour_sum / neighbour_count[:, None, None]
    )
    balanced = centred.astype(jnp.bfloat16)
    magnitude = jnp.abs(balanced)
    sample_index = jnp.arange(samples, dtype=jnp.int32)
    ram_band = jnp.abs(sample_index[:, None] - sample_index[None, :]) <= ram_half
    ram_count = jnp.sum(ram_band.astype(jnp.float32), axis=0)
    ram_sum = jnp.einsum(
        "cwl,lm->cwm", magnitude, ram_band.astype(jnp.bfloat16), preferred_element_type=jnp.float32
    )
    envelope = ram_sum / ram_count + epsilon
    normalized = (balanced.astype(jnp.float32) / envelope).astype(jnp.bfloat16)
    frequency = jnp.arange(1, bin_count + 1, dtype=jnp.int32)
    phase_steps = frequency[:, None] * sample_index[None, :] % samples
    phase = 2.0 * math.pi / samples * phase_steps.astype(jnp.float32)
    dft_table = (
        jnp.concatenate([jnp.cos(phase), -jnp.sin(phase)], axis=0) / math.sqrt(samples)
    ).astype(jnp.bfloat16)
    spectra = jnp.einsum("jl,cwl->jwc", dft_table, normalized, preferred_element_type=jnp.float32)
    spectra = spectra.reshape(2, bin_count, window_count, channel_count)
    power_bins = spectra[0] * spectra[0] + spectra[1] * spectra[1]
    same_band = (bands[:, None] == bands[None, :]).astype(jnp.float32)
    band_matrix = same_band / jnp.sum(same_band, axis=1, keepdims=True)
    band_mean = jnp.einsum("fg,gwc->fwc", band_matrix, power_bins, precision=lax.Precision.HIGHEST)
    whiten_scale = lax.rsqrt(jnp.maximum(band_mean, floor_power))
    return (spectra * whiten_scale[None]).astype(jnp.bfloat16)


def whiten_block(block, sel, count, ram, ram_count, table, band):
    halo = (block.shape[0] - sel.shape[0]) // 2
    channels = sel.shape[0]
    bins = band.shape[0]
    block = jnp.swapaxes(block.astype(jnp.float32), 0, 1)
    rows = []
    for w in range(block.shape[0]):
        x = block[w]
        neighbour_sum = jnp.dot(sel, x.astype(jnp.bfloat16), preferred_element_type=jnp.float32)
        balanced = (x[halo : halo + channels] - neighbour_sum / count).astype(jnp.bfloat16)
        ram_sum = jnp.dot(jnp.abs(balanced), ram, preferred_element_type=jnp.float32)
        envelope = ram_sum / ram_count + epsilon
        normalized = (balanced.astype(jnp.float32) / envelope).astype(jnp.bfloat16)
        spectra = lax.dot_general(
            table, normalized, (((1,), (1,)), ((), ())), preferred_element_type=jnp.float32
        )
        real, imag = spectra[:bins], spectra[bins:]
        power = real * real + imag * imag
        band_mean = jnp.dot(band, power, precision=lax.Precision.HIGHEST, preferred_element_type=jnp.float32)
        scale = lax.rsqrt(jnp.maximum(band_mean, floor_power))
        rows.append(jnp.concatenate([real * scale, imag * scale], axis=0))
    whitened = jnp.swapaxes(jnp.stack(rows, axis=0), 0, 1)
    return whitened.reshape(2, bins, whitened.shape[1], channels)


def prepare_kernel(ext_ref, sel_ref, count_ref, ram_ref, ram_count_ref, table_ref, band_ref, out_ref):
    consts = [r[...] for r in (sel_ref, count_ref, ram_ref, ram_count_ref, table_ref, band_ref)]
    out_ref[...] = whiten_block(ext_ref[...], *consts).astype(out_ref.dtype)


def constants(first_channel, total_channels, bands, channel_count, halo_width, samples, ram_half):
    ext_rows = channel_count + 2 * halo_width
    bin_count = samples // 2
    inner = jnp.arange(channel_count, dtype=jnp.int32)
    outer = jnp.arange(ext_rows, dtype=jnp.int32)
    offset = outer[None, :] - inner[:, None]
    outer_position = first_channel - halo_width + outer
    inside = (outer_position >= 0) & (outer_position < total_channels)
    selector = (offset >= 0) & (offset <= 2 * halo_width) & inside[None, :]
    neighbour_count = jnp.sum(selector.astype(jnp.float32), axis=1)[:, None]
    sample_index = jnp.arange(samples, dtype=jnp.int32)
    ram_band = jnp.abs(sample_index[:, None] - sample_index[None, :]) <= ram_half
    ram_count = jnp.sum(ram_band.astype(jnp.float32), axis=0)[None, :]
    frequency = jnp.arange(1, bin_count + 1, dtype=jnp.int32)
    phase_steps = frequency[:, None] * sample_index[None, :] % samples
    phase = 2.0 * math.pi / samples * phase_steps.astype(jnp.float32)
    dft_table = (
        jnp.concatenate([jnp.cos(phase), -jnp.sin(phase)], axis=0) / math.sqrt(samples)
    ).astype(jnp.bfloat16)
    same_band = (bands[:, None] == bands[None, :]).astype(jnp.float32)
    band_matrix = same_band / jnp.sum(same_band, axis=1, keepdims=True)
    return [
        selector.astype(jnp.bfloat16),
        neighbour_count,
        ram_band.astype(jnp.bfloat16),
        ram_count,
        dft_table,
        band_matrix,
    ]


def prepare_fast(extended, consts, windows, step=16):
    ext_rows, _, samples = extended.shape
    channel_count = consts[0].shape[0]
    bin_count = samples // 2
    whole = lambda i: (0, 0)
    return pl.pallas_call(
        prepare_kernel,
        out_shape=jax.ShapeDtypeStruct((2, bin_count, windows, channel_count), jnp.bfloat16),
        grid=(windows // step,),
        in_specs=[pl.BlockSpec((ext_rows, step, samples), lambda i: (0, i, 0))]
        + [pl.BlockSpec(c.shape, whole) for c in consts],
        out_specs=pl.BlockSpec((2, bin_count, step, channel_count), lambda i: (0, 0, i, 0)),
    )(extended, *consts)


def correlate_chunk(owns, partners, out, r, rows, scale):
    dims = (((0,), (0,)), ((), ()))
    real_rows, imag_rows = [], []
    for j in range(rows.size):
        f = rows.start + j
        real, imag = 0.0, 0.0
        for own, partner in zip(owns, partners):
            x = own[:, f]
            y = partner[:, f]
            lhs = x.reshape(-1, x.shape[-1])
            real_rhs = y.reshape(-1, y.shape[-1])
            imag_rhs = jnp.concatenate([-y[1], y[0]], axis=0)
            rhs = jnp.concatenate([real_rhs, imag_rhs], axis=1)
            both = lax.dot_general(lhs, rhs, dims, preferred_element_type=jnp.float32)
            real = real + both[:, : y.shape[-1]]
            imag = imag + both[:, y.shape[-1] :]
        real_rows.append(real / scale)
        imag_rows.append(imag / scale)
    out[:, r, 0, rows, :] = jnp.stack(real_rows, axis=1).astype(out.dtype)
    out[:, r, 1, rows, :] = jnp.stack(imag_rows, axis=1).astype(out.dtype)


def exchange_kernel(n, chunks, scale, step, bounds, early, ext, sel, count, ram, ram_count, table, band,
                    out, lates, first, second, first_send, first_recv, second_send, second_recv):
    me = lax.axis_index("blk")
    core = lax.rem(me, 2)
    down = lax.rem(me + n - 2, n)
    up = lax.rem(me + 2, n)
    mate = me + 1 - 2 * core

    barrier = pltpu.get_barrier_semaphore()
    for peer in (down, up, mate):
        pl.semaphore_signal(barrier, inc=1, device_id=(peer,), device_id_type=MESH)
    pl.semaphore_wait(barrier, 3)

    size = early.shape[1] // chunks
    owns = [early] + list(lates)

    def part(i):
        return pl.ds(pl.multiple_of(i * size, size), size)

    def to_down(p, i):
        return pltpu.make_async_remote_copy(
            owns[p].at[:, part(i)], second[p].at[:, part(i)], second_send.at[p, i], second_recv.at[p, i],
            device_id=(down,), device_id_type=MESH)

    def to_mate(src, p, i):
        return pltpu.make_async_remote_copy(
            src.at[:, part(i)], first[p].at[:, part(i)], first_send.at[p, i], first_recv.at[p, i],
            device_id=(mate,), device_id_type=MESH)

    def send_part(p):
        @pl.loop(0, chunks)
        def _(i):
            to_down(p, i).start()

        @pl.when(core == 1)
        def _():
            @pl.loop(0, chunks)
            def _(i):
                to_mate(owns[p], p, i).start()

    send_part(0)
    consts = [r[...] for r in (sel, count, ram, ram_count, table, band)]
    for p, (start, length) in enumerate(bounds, start=1):
        late = lates[p - 1]

        @pl.loop(0, length // step)
        def _(b):
            src = pl.ds(pl.multiple_of(start + b * step, step), step)
            dst = pl.ds(pl.multiple_of(b * step, step), step)
            late[:, :, dst, :] = whiten_block(ext[:, src, :], *consts).astype(late.dtype)

        send_part(p)

    parts = len(owns)

    @pl.loop(0, chunks)
    def _(i):
        for p in range(parts):
            to_down(p, i).wait_recv()

            @pl.when(core == 0)
            def _():
                to_mate(second[p], p, i).start()

        correlate_chunk(owns, second, out, 1, part(i), scale)
        for p in range(parts):
            to_mate(second[p], p, i).wait_recv()
        correlate_chunk(owns, first, out, 0, part(i), scale)

    @pl.loop(0, chunks)
    def _(i):
        for p in range(parts):
            to_down(p, i).wait_send()
            to_mate(second[p], p, i).wait_send()


def per_device(traces, bands, chunks=4, split=(16, 32, 48, 48), step=16):
    extended = with_halo(traces, (("blk", 0),), HW)
    channel_count, window_count, samples = traces.shape
    n = lax.axis_size("blk")
    first_channel = lax.axis_index("blk") * channel_count
    consts = constants(first_channel, channel_count * n, bands, channel_count, HW, samples, RAM_HALF)
    early = prepare_fast(extended, consts, split[0], step)
    bounds, start = [], split[0]
    for length in split[1:]:
        bounds.append((start, length))
        start += length
    bins = samples // 2
    shapes = [(2, bins, length, channel_count) for length in split]
    buffers = lambda: [pltpu.VMEM(shape, jnp.bfloat16) for shape in shapes]
    vmem = pl.BlockSpec(memory_space=pltpu.VMEM)
    parts = len(split)
    return pl.pallas_call(
        functools.partial(exchange_kernel, n, chunks, math.sqrt(window_count), step, bounds),
        out_shape=jax.ShapeDtypeStruct((channel_count, ROUNDS, 2, bins, channel_count), jnp.bfloat16),
        in_specs=[vmem] * 8,
        out_specs=vmem,
        scratch_shapes=[
            buffers()[1:],
            buffers(),
            buffers(),
            pltpu.SemaphoreType.DMA((parts, chunks)),
            pltpu.SemaphoreType.DMA((parts, chunks)),
            pltpu.SemaphoreType.DMA((parts, chunks)),
            pltpu.SemaphoreType.DMA((parts, chunks)),
        ],
        compiler_params=pltpu.CompilerParams(
            collective_id=0, has_side_effects=True, vmem_limit_bytes=60 * 1024 * 1024
        ),
    )(early, extended, *consts)


def solution(mesh):
    placed = (P("blk", None, None), P())
    return jax.shard_map(
        per_device,
        mesh=mesh,
        in_specs=placed,
        out_specs=P("blk", None, None, None, None),
        check_vma=False,
    )
```

```python
import functools
import math

import jax
import jax.numpy as jnp
from jax import lax
from jax.experimental import pallas as pl
from jax.experimental.pallas import tpu as pltpu
from jax.sharding import PartitionSpec as P

MESH = pl.DeviceIdType.MESH

HW = 16
RAM_HALF = 64
ROUNDS = 2


epsilon = 1e-05
floor_power = 0.25


def with_halo(cells, sides, width):
    for axis, dim in sides:
        count = lax.axis_size(axis)
        ends = count - 1
        head = lax.slice_in_dim(cells, 0, width, axis=dim)
        tail = lax.slice_in_dim(cells, cells.shape[dim] - width, cells.shape[dim], axis=dim)
        cells = jnp.concatenate(
            [
                lax.ppermute(tail, axis, [(i, (i + 1) % count) for i in range(ends)]),
                cells,
                lax.ppermute(head, axis, [((i + 1) % count, i) for i in range(ends)]),
            ],
            axis=dim,
        )
    return cells


def shifted(shard, axis, by):
    count = lax.axis_size(axis)
    return lax.ppermute(shard, axis, [(i, (i + by) % count) for i in range(count)])


def prepare(extended, first_channel, total_channels, bands, halo_width, ram_half):
    channel_count = extended.shape[0] - 2 * halo_width
    ext_rows = extended.shape[0]
    window_count = extended.shape[1]
    samples = extended.shape[2]
    bin_count = samples // 2
    inner = jnp.arange(channel_count, dtype=jnp.int32)
    outer = jnp.arange(ext_rows, dtype=jnp.int32)
    offset = outer[None, :] - inner[:, None]
    outer_position = first_channel - halo_width + outer
    inside = (outer_position >= 0) & (outer_position < total_channels)
    selector = (offset >= 0) & (offset <= 2 * halo_width) & inside[None, :]
    neighbour_count = jnp.sum(selector.astype(jnp.float32), axis=1)
    neighbour_sum = jnp.einsum(
        "ie,ewl->iwl", selector.astype(jnp.bfloat16), extended, preferred_element_type=jnp.float32
    )
    centred = (
        extended[halo_width : halo_width + channel_count].astype(jnp.float32)
        - neighbour_sum / neighbour_count[:, None, None]
    )
    balanced = centred.astype(jnp.bfloat16)
    magnitude = jnp.abs(balanced)
    sample_index = jnp.arange(samples, dtype=jnp.int32)
    ram_band = jnp.abs(sample_index[:, None] - sample_index[None, :]) <= ram_half
    ram_count = jnp.sum(ram_band.astype(jnp.float32), axis=0)
    ram_sum = jnp.einsum(
        "cwl,lm->cwm", magnitude, ram_band.astype(jnp.bfloat16), preferred_element_type=jnp.float32
    )
    envelope = ram_sum / ram_count + epsilon
    normalized = (balanced.astype(jnp.float32) / envelope).astype(jnp.bfloat16)
    frequency = jnp.arange(1, bin_count + 1, dtype=jnp.int32)
    phase_steps = frequency[:, None] * sample_index[None, :] % samples
    phase = 2.0 * math.pi / samples * phase_steps.astype(jnp.float32)
    dft_table = (
        jnp.concatenate([jnp.cos(phase), -jnp.sin(phase)], axis=0) / math.sqrt(samples)
    ).astype(jnp.bfloat16)
    spectra = jnp.einsum("jl,cwl->jwc", dft_table, normalized, preferred_element_type=jnp.float32)
    spectra = spectra.reshape(2, bin_count, window_count, channel_count)
    power_bins = spectra[0] * spectra[0] + spectra[1] * spectra[1]
    same_band = (bands[:, None] == bands[None, :]).astype(jnp.float32)
    band_matrix = same_band / jnp.sum(same_band, axis=1, keepdims=True)
    band_mean = jnp.einsum("fg,gwc->fwc", band_matrix, power_bins, precision=lax.Precision.HIGHEST)
    whiten_scale = lax.rsqrt(jnp.maximum(band_mean, floor_power))
    return (spectra * whiten_scale[None]).astype(jnp.bfloat16)


def whiten_block(block, sel, count, ram, ram_count, table, band):
    halo = (block.shape[0] - sel.shape[0]) // 2
    channels = sel.shape[0]
    bins = band.shape[0]
    block = jnp.swapaxes(block.astype(jnp.float32), 0, 1)
    rows = []
    for w in range(block.shape[0]):
        x = block[w]
        neighbour_sum = jnp.dot(sel, x.astype(jnp.bfloat16), preferred_element_type=jnp.float32)
        balanced = (x[halo : halo + channels] - neighbour_sum / count).astype(jnp.bfloat16)
        ram_sum = jnp.dot(jnp.abs(balanced), ram, preferred_element_type=jnp.float32)
        envelope = ram_sum / ram_count + epsilon
        normalized = (balanced.astype(jnp.float32) / envelope).astype(jnp.bfloat16)
        spectra = lax.dot_general(
            table, normalized, (((1,), (1,)), ((), ())), preferred_element_type=jnp.float32
        )
        real, imag = spectra[:bins], spectra[bins:]
        power = real * real + imag * imag
        band_mean = jnp.dot(band, power, precision=lax.Precision.HIGHEST, preferred_element_type=jnp.float32)
        scale = lax.rsqrt(jnp.maximum(band_mean, floor_power))
        rows.append(jnp.concatenate([real * scale, imag * scale], axis=0))
    whitened = jnp.swapaxes(jnp.stack(rows, axis=0), 0, 1)
    return whitened.reshape(2, bins, whitened.shape[1], channels)


def prepare_kernel(ext_ref, sel_ref, count_ref, ram_ref, ram_count_ref, table_ref, band_ref, out_ref):
    consts = [r[...] for r in (sel_ref, count_ref, ram_ref, ram_count_ref, table_ref, band_ref)]
    out_ref[...] = whiten_block(ext_ref[...], *consts).astype(out_ref.dtype)


def constants(first_channel, total_channels, bands, channel_count, halo_width, samples, ram_half):
    ext_rows = channel_count + 2 * halo_width
    bin_count = samples // 2
    inner = jnp.arange(channel_count, dtype=jnp.int32)
    outer = jnp.arange(ext_rows, dtype=jnp.int32)
    offset = outer[None, :] - inner[:, None]
    outer_position = first_channel - halo_width + outer
    inside = (outer_position >= 0) & (outer_position < total_channels)
    selector = (offset >= 0) & (offset <= 2 * halo_width) & inside[None, :]
    neighbour_count = jnp.sum(selector.astype(jnp.float32), axis=1)[:, None]
    sample_index = jnp.arange(samples, dtype=jnp.int32)
    ram_band = jnp.abs(sample_index[:, None] - sample_index[None, :]) <= ram_half
    ram_count = jnp.sum(ram_band.astype(jnp.float32), axis=0)[None, :]
    frequency = jnp.arange(1, bin_count + 1, dtype=jnp.int32)
    phase_steps = frequency[:, None] * sample_index[None, :] % samples
    phase = 2.0 * math.pi / samples * phase_steps.astype(jnp.float32)
    dft_table = (
        jnp.concatenate([jnp.cos(phase), -jnp.sin(phase)], axis=0) / math.sqrt(samples)
    ).astype(jnp.bfloat16)
    same_band = (bands[:, None] == bands[None, :]).astype(jnp.float32)
    band_matrix = same_band / jnp.sum(same_band, axis=1, keepdims=True)
    return [
        selector.astype(jnp.bfloat16),
        neighbour_count,
        ram_band.astype(jnp.bfloat16),
        ram_count,
        dft_table,
        band_matrix,
    ]


def prepare_fast(extended, consts, windows, step=16):
    ext_rows, _, samples = extended.shape
    channel_count = consts[0].shape[0]
    bin_count = samples // 2
    whole = lambda i: (0, 0)
    return pl.pallas_call(
        prepare_kernel,
        out_shape=jax.ShapeDtypeStruct((2, bin_count, windows, channel_count), jnp.bfloat16),
        grid=(windows // step,),
        in_specs=[pl.BlockSpec((ext_rows, step, samples), lambda i: (0, i, 0))]
        + [pl.BlockSpec(c.shape, whole) for c in consts],
        out_specs=pl.BlockSpec((2, bin_count, step, channel_count), lambda i: (0, 0, i, 0)),
    )(extended, *consts)


def correlate_chunk(own, partner, acc, out, r, rows, scale, mode):
    dims = (((0,), (0,)), ((), ()))
    width = own.shape[-1]
    real_rows, imag_rows = [], []
    for j in range(rows.size):
        f = rows.start + j
        x = own[:, f]
        y = partner[:, f]
        lhs = x.reshape(-1, x.shape[-1])
        real_rhs = y.reshape(-1, y.shape[-1])
        imag_rhs = jnp.concatenate([-y[1], y[0]], axis=0)
        rhs = jnp.concatenate([real_rhs, imag_rhs], axis=1)
        both = lax.dot_general(lhs, rhs, dims, preferred_element_type=jnp.float32)
        if mode == "first":
            acc[r, f] = both
        elif mode == "middle":
            acc[r, f] = acc[r, f] + both
        else:
            total = acc[r, f] + both
            real_rows.append(total[:, :width] / scale)
            imag_rows.append(total[:, width:] / scale)
    if mode == "last":
        out[:, r, 0, rows, :] = jnp.stack(real_rows, axis=1).astype(out.dtype)
        out[:, r, 1, rows, :] = jnp.stack(imag_rows, axis=1).astype(out.dtype)


def exchange_kernel(n, chunks, scale, step, bounds, early, ext, sel, count, ram, ram_count, table, band,
                    out, lates, first, second, acc, first_send, first_recv, second_send, second_recv):
    me = lax.axis_index("blk")
    core = lax.rem(me, 2)
    down = lax.rem(me + n - 2, n)
    up = lax.rem(me + 2, n)
    mate = me + 1 - 2 * core

    barrier = pltpu.get_barrier_semaphore()
    for peer in (down, up, mate):
        pl.semaphore_signal(barrier, inc=1, device_id=(peer,), device_id_type=MESH)
    pl.semaphore_wait(barrier, 3)

    size = early.shape[1] // chunks
    owns = [early] + list(lates)

    def part(i):
        return pl.ds(pl.multiple_of(i * size, size), size)

    def to_down(p, i):
        return pltpu.make_async_remote_copy(
            owns[p].at[:, part(i)], second[p].at[:, part(i)], second_send.at[p, i], second_recv.at[p, i],
            device_id=(down,), device_id_type=MESH)

    def to_mate(src, p, i):
        return pltpu.make_async_remote_copy(
            src.at[:, part(i)], first[p].at[:, part(i)], first_send.at[p, i], first_recv.at[p, i],
            device_id=(mate,), device_id_type=MESH)

    def send_part(p):
        @pl.loop(0, chunks)
        def _(i):
            to_down(p, i).start()

        @pl.when(core == 1)
        def _():
            @pl.loop(0, chunks)
            def _(i):
                to_mate(owns[p], p, i).start()

    send_part(0)
    consts = [r[...] for r in (sel, count, ram, ram_count, table, band)]
    for p, (start, length) in enumerate(bounds, start=1):
        late = lates[p - 1]

        @pl.loop(0, length // step)
        def _(b):
            src = pl.ds(pl.multiple_of(start + b * step, step), step)
            dst = pl.ds(pl.multiple_of(b * step, step), step)
            late[:, :, dst, :] = whiten_block(ext[:, src, :], *consts).astype(late.dtype)

        send_part(p)

    parts = len(owns)
    for p in range(parts):
        mode = "first" if p == 0 else ("last" if p == parts - 1 else "middle")

        @pl.loop(0, chunks)
        def _(i):
            to_down(p, i).wait_recv()

            @pl.when(core == 0)
            def _():
                to_mate(second[p], p, i).start()

            correlate_chunk(owns[p], second[p], acc, out, 1, part(i), scale, mode)
            to_mate(second[p], p, i).wait_recv()
            correlate_chunk(owns[p], first[p], acc, out, 0, part(i), scale, mode)

    @pl.loop(0, chunks)
    def _(i):
        for p in range(parts):
            to_down(p, i).wait_send()
            to_mate(second[p], p, i).wait_send()


def per_device(traces, bands, chunks=4, split=(16, 32, 48, 48), step=16):
    extended = with_halo(traces, (("blk", 0),), HW)
    channel_count, window_count, samples = traces.shape
    n = lax.axis_size("blk")
    first_channel = lax.axis_index("blk") * channel_count
    consts = constants(first_channel, channel_count * n, bands, channel_count, HW, samples, RAM_HALF)
    early = prepare_fast(extended, consts, split[0], step)
    bounds, start = [], split[0]
    for length in split[1:]:
        bounds.append((start, length))
        start += length
    bins = samples // 2
    shapes = [(2, bins, length, channel_count) for length in split]
    buffers = lambda: [pltpu.VMEM(shape, jnp.bfloat16) for shape in shapes]
    vmem = pl.BlockSpec(memory_space=pltpu.VMEM)
    parts = len(split)
    return pl.pallas_call(
        functools.partial(exchange_kernel, n, chunks, math.sqrt(window_count), step, bounds),
        out_shape=jax.ShapeDtypeStruct((channel_count, ROUNDS, 2, bins, channel_count), jnp.bfloat16),
        in_specs=[vmem] * 8,
        out_specs=vmem,
        scratch_shapes=[
            buffers()[1:],
            buffers(),
            buffers(),
            pltpu.VMEM((ROUNDS, bins, channel_count, 2 * channel_count), jnp.float32),
            pltpu.SemaphoreType.DMA((parts, chunks)),
            pltpu.SemaphoreType.DMA((parts, chunks)),
            pltpu.SemaphoreType.DMA((parts, chunks)),
            pltpu.SemaphoreType.DMA((parts, chunks)),
        ],
        compiler_params=pltpu.CompilerParams(
            collective_id=0, has_side_effects=True, vmem_limit_bytes=63 * 1024 * 1024
        ),
    )(early, extended, *consts)


def solution(mesh):
    placed = (P("blk", None, None), P())
    return jax.shard_map(
        per_device,
        mesh=mesh,
        in_specs=placed,
        out_specs=P("blk", None, None, None, None),
        check_vma=False,
    )
```

```python
import functools
import math

import jax
import jax.numpy as jnp
from jax import lax
from jax.experimental import pallas as pl
from jax.experimental.pallas import tpu as pltpu
from jax.sharding import PartitionSpec as P

MESH = pl.DeviceIdType.MESH

HW = 16
RAM_HALF = 64
ROUNDS = 2


epsilon = 1e-05
floor_power = 0.25


def with_halo(cells, sides, width):
    for axis, dim in sides:
        count = lax.axis_size(axis)
        ends = count - 1
        head = lax.slice_in_dim(cells, 0, width, axis=dim)
        tail = lax.slice_in_dim(cells, cells.shape[dim] - width, cells.shape[dim], axis=dim)
        cells = jnp.concatenate(
            [
                lax.ppermute(tail, axis, [(i, (i + 1) % count) for i in range(ends)]),
                cells,
                lax.ppermute(head, axis, [((i + 1) % count, i) for i in range(ends)]),
            ],
            axis=dim,
        )
    return cells


def shifted(shard, axis, by):
    count = lax.axis_size(axis)
    return lax.ppermute(shard, axis, [(i, (i + by) % count) for i in range(count)])


def prepare(extended, first_channel, total_channels, bands, halo_width, ram_half):
    channel_count = extended.shape[0] - 2 * halo_width
    ext_rows = extended.shape[0]
    window_count = extended.shape[1]
    samples = extended.shape[2]
    bin_count = samples // 2
    inner = jnp.arange(channel_count, dtype=jnp.int32)
    outer = jnp.arange(ext_rows, dtype=jnp.int32)
    offset = outer[None, :] - inner[:, None]
    outer_position = first_channel - halo_width + outer
    inside = (outer_position >= 0) & (outer_position < total_channels)
    selector = (offset >= 0) & (offset <= 2 * halo_width) & inside[None, :]
    neighbour_count = jnp.sum(selector.astype(jnp.float32), axis=1)
    neighbour_sum = jnp.einsum(
        "ie,ewl->iwl", selector.astype(jnp.bfloat16), extended, preferred_element_type=jnp.float32
    )
    centred = (
        extended[halo_width : halo_width + channel_count].astype(jnp.float32)
        - neighbour_sum / neighbour_count[:, None, None]
    )
    balanced = centred.astype(jnp.bfloat16)
    magnitude = jnp.abs(balanced)
    sample_index = jnp.arange(samples, dtype=jnp.int32)
    ram_band = jnp.abs(sample_index[:, None] - sample_index[None, :]) <= ram_half
    ram_count = jnp.sum(ram_band.astype(jnp.float32), axis=0)
    ram_sum = jnp.einsum(
        "cwl,lm->cwm", magnitude, ram_band.astype(jnp.bfloat16), preferred_element_type=jnp.float32
    )
    envelope = ram_sum / ram_count + epsilon
    normalized = (balanced.astype(jnp.float32) / envelope).astype(jnp.bfloat16)
    frequency = jnp.arange(1, bin_count + 1, dtype=jnp.int32)
    phase_steps = frequency[:, None] * sample_index[None, :] % samples
    phase = 2.0 * math.pi / samples * phase_steps.astype(jnp.float32)
    dft_table = (
        jnp.concatenate([jnp.cos(phase), -jnp.sin(phase)], axis=0) / math.sqrt(samples)
    ).astype(jnp.bfloat16)
    spectra = jnp.einsum("jl,cwl->jwc", dft_table, normalized, preferred_element_type=jnp.float32)
    spectra = spectra.reshape(2, bin_count, window_count, channel_count)
    power_bins = spectra[0] * spectra[0] + spectra[1] * spectra[1]
    same_band = (bands[:, None] == bands[None, :]).astype(jnp.float32)
    band_matrix = same_band / jnp.sum(same_band, axis=1, keepdims=True)
    band_mean = jnp.einsum("fg,gwc->fwc", band_matrix, power_bins, precision=lax.Precision.HIGHEST)
    whiten_scale = lax.rsqrt(jnp.maximum(band_mean, floor_power))
    return (spectra * whiten_scale[None]).astype(jnp.bfloat16)


def whiten_block(block, sel, count, ram, ram_count, table, band):
    halo = (block.shape[0] - sel.shape[0]) // 2
    channels = sel.shape[0]
    bins = band.shape[0]
    block = jnp.swapaxes(block.astype(jnp.float32), 0, 1)
    rows = []
    for w in range(block.shape[0]):
        x = block[w]
        neighbour_sum = jnp.dot(sel, x.astype(jnp.bfloat16), preferred_element_type=jnp.float32)
        balanced = (x[halo : halo + channels] - neighbour_sum / count).astype(jnp.bfloat16)
        ram_sum = jnp.dot(jnp.abs(balanced), ram, preferred_element_type=jnp.float32)
        envelope = ram_sum / ram_count + epsilon
        normalized = (balanced.astype(jnp.float32) / envelope).astype(jnp.bfloat16)
        spectra = lax.dot_general(
            table, normalized, (((1,), (1,)), ((), ())), preferred_element_type=jnp.float32
        )
        real, imag = spectra[:bins], spectra[bins:]
        power = real * real + imag * imag
        band_mean = jnp.dot(band, power, precision=lax.Precision.HIGHEST, preferred_element_type=jnp.float32)
        scale = lax.rsqrt(jnp.maximum(band_mean, floor_power))
        rows.append(jnp.concatenate([real * scale, imag * scale], axis=0))
    whitened = jnp.swapaxes(jnp.stack(rows, axis=0), 0, 1)
    return whitened.reshape(2, bins, whitened.shape[1], channels)


def prepare_kernel(ext_ref, sel_ref, count_ref, ram_ref, ram_count_ref, table_ref, band_ref, out_ref):
    consts = [r[...] for r in (sel_ref, count_ref, ram_ref, ram_count_ref, table_ref, band_ref)]
    out_ref[...] = whiten_block(ext_ref[...], *consts).astype(out_ref.dtype)


def constants(first_channel, total_channels, bands, channel_count, halo_width, samples, ram_half):
    ext_rows = channel_count + 2 * halo_width
    bin_count = samples // 2
    inner = jnp.arange(channel_count, dtype=jnp.int32)
    outer = jnp.arange(ext_rows, dtype=jnp.int32)
    offset = outer[None, :] - inner[:, None]
    outer_position = first_channel - halo_width + outer
    inside = (outer_position >= 0) & (outer_position < total_channels)
    selector = (offset >= 0) & (offset <= 2 * halo_width) & inside[None, :]
    neighbour_count = jnp.sum(selector.astype(jnp.float32), axis=1)[:, None]
    sample_index = jnp.arange(samples, dtype=jnp.int32)
    ram_band = jnp.abs(sample_index[:, None] - sample_index[None, :]) <= ram_half
    ram_count = jnp.sum(ram_band.astype(jnp.float32), axis=0)[None, :]
    frequency = jnp.arange(1, bin_count + 1, dtype=jnp.int32)
    phase_steps = frequency[:, None] * sample_index[None, :] % samples
    phase = 2.0 * math.pi / samples * phase_steps.astype(jnp.float32)
    dft_table = (
        jnp.concatenate([jnp.cos(phase), -jnp.sin(phase)], axis=0) / math.sqrt(samples)
    ).astype(jnp.bfloat16)
    same_band = (bands[:, None] == bands[None, :]).astype(jnp.float32)
    band_matrix = same_band / jnp.sum(same_band, axis=1, keepdims=True)
    return [
        selector.astype(jnp.bfloat16),
        neighbour_count,
        ram_band.astype(jnp.bfloat16),
        ram_count,
        dft_table,
        band_matrix,
    ]


def prepare_fast(extended, consts, windows, step=16):
    ext_rows, _, samples = extended.shape
    channel_count = consts[0].shape[0]
    bin_count = samples // 2
    whole = lambda i: (0, 0)
    return pl.pallas_call(
        prepare_kernel,
        out_shape=jax.ShapeDtypeStruct((2, bin_count, windows, channel_count), jnp.bfloat16),
        grid=(windows // step,),
        in_specs=[pl.BlockSpec((ext_rows, step, samples), lambda i: (0, i, 0))]
        + [pl.BlockSpec(c.shape, whole) for c in consts],
        out_specs=pl.BlockSpec((2, bin_count, step, channel_count), lambda i: (0, 0, i, 0)),
    )(extended, *consts)


def correlate_chunk(own, partner, acc, out, r, rows, scale, mode):
    dims = (((0,), (0,)), ((), ()))
    width = own.shape[-1]
    real_rows, imag_rows = [], []
    for j in range(rows.size):
        f = rows.start + j
        x = own[:, f]
        y = partner[:, f]
        lhs = x.reshape(-1, x.shape[-1])
        real_rhs = y.reshape(-1, y.shape[-1])
        imag_rhs = jnp.concatenate([-y[1], y[0]], axis=0)
        rhs = jnp.concatenate([real_rhs, imag_rhs], axis=1)
        both = lax.dot_general(lhs, rhs, dims, preferred_element_type=jnp.float32)
        if mode == "first":
            acc[r, f] = both
        elif mode == "middle":
            acc[r, f] = acc[r, f] + both
        else:
            total = acc[r, f] + both
            real_rows.append(total[:, :width] / scale)
            imag_rows.append(total[:, width:] / scale)
    if mode == "last":
        out[:, r, 0, rows, :] = jnp.stack(real_rows, axis=1).astype(out.dtype)
        out[:, r, 1, rows, :] = jnp.stack(imag_rows, axis=1).astype(out.dtype)


def exchange_kernel(n, chunks, scale, step, bounds, traces, sel, count, ram, ram_count, table, band,
                    out, head, tail, owns, first, second, acc, halo_send, halo_recv,
                    first_send, first_recv, second_send, second_recv):
    me = lax.axis_index("blk")
    core = lax.rem(me, 2)
    down = lax.rem(me + n - 2, n)
    up = lax.rem(me + 2, n)
    left = lax.rem(me + n - 1, n)
    right = lax.rem(me + 1, n)
    mate = me + 1 - 2 * core
    halo = head.shape[0]
    channels = traces.shape[0]

    barrier = pltpu.get_barrier_semaphore()
    for peer in (down, up, left, right):
        pl.semaphore_signal(barrier, inc=1, device_id=(peer,), device_id_type=MESH)
    pl.semaphore_wait(barrier, 4)

    to_right = pltpu.make_async_remote_copy(
        traces.at[pl.ds(channels - halo, halo)], head, halo_send.at[0], halo_recv.at[0],
        device_id=(right,), device_id_type=MESH)
    to_left = pltpu.make_async_remote_copy(
        traces.at[pl.ds(0, halo)], tail, halo_send.at[1], halo_recv.at[1],
        device_id=(left,), device_id_type=MESH)
    to_right.start()
    to_left.start()

    size = owns[0].shape[1] // chunks

    def part(i):
        return pl.ds(pl.multiple_of(i * size, size), size)

    def to_down(p, i):
        return pltpu.make_async_remote_copy(
            owns[p].at[:, part(i)], second[p].at[:, part(i)], second_send.at[p, i], second_recv.at[p, i],
            device_id=(down,), device_id_type=MESH)

    def to_mate(src, p, i):
        return pltpu.make_async_remote_copy(
            src.at[:, part(i)], first[p].at[:, part(i)], first_send.at[p, i], first_recv.at[p, i],
            device_id=(mate,), device_id_type=MESH)

    def send_part(p):
        @pl.loop(0, chunks)
        def _(i):
            to_down(p, i).start()

        @pl.when(core == 1)
        def _():
            @pl.loop(0, chunks)
            def _(i):
                to_mate(owns[p], p, i).start()

    consts = [r[...] for r in (sel, count, ram, ram_count, table, band)]
    to_right.wait_recv()
    to_left.wait_recv()
    for p, (start, length) in enumerate(bounds):
        late = owns[p]

        @pl.loop(0, length // step)
        def _(b):
            src = pl.ds(pl.multiple_of(start + b * step, step), step)
            dst = pl.ds(pl.multiple_of(b * step, step), step)
            block = jnp.concatenate([head[:, src, :], traces[:, src, :], tail[:, src, :]], axis=0)
            late[:, :, dst, :] = whiten_block(block, *consts).astype(late.dtype)

        send_part(p)

    parts = len(owns)
    for p in range(parts):
        mode = "first" if p == 0 else ("last" if p == parts - 1 else "middle")

        @pl.loop(0, chunks)
        def _(i):
            to_down(p, i).wait_recv()

            @pl.when(core == 0)
            def _():
                to_mate(second[p], p, i).start()

            correlate_chunk(owns[p], second[p], acc, out, 1, part(i), scale, mode)
            to_mate(second[p], p, i).wait_recv()
            correlate_chunk(owns[p], first[p], acc, out, 0, part(i), scale, mode)

    to_right.wait_send()
    to_left.wait_send()

    @pl.loop(0, chunks)
    def _(i):
        for p in range(parts):
            to_down(p, i).wait_send()
            to_mate(second[p], p, i).wait_send()


def per_device(traces, bands, chunks=4, split=(16, 32, 48, 48), step=16):
    channel_count, window_count, samples = traces.shape
    n = lax.axis_size("blk")
    first_channel = lax.axis_index("blk") * channel_count
    consts = constants(first_channel, channel_count * n, bands, channel_count, HW, samples, RAM_HALF)
    bounds, start = [], 0
    for length in split:
        bounds.append((start, length))
        start += length
    bins = samples // 2
    shapes = [(2, bins, length, channel_count) for length in split]
    buffers = lambda: [pltpu.VMEM(shape, jnp.bfloat16) for shape in shapes]
    vmem = pl.BlockSpec(memory_space=pltpu.VMEM)
    parts = len(split)
    return pl.pallas_call(
        functools.partial(exchange_kernel, n, chunks, math.sqrt(window_count), step, bounds),
        out_shape=jax.ShapeDtypeStruct((channel_count, ROUNDS, 2, bins, channel_count), jnp.bfloat16),
        in_specs=[vmem] * 7,
        out_specs=vmem,
        scratch_shapes=[
            pltpu.VMEM((HW, window_count, samples), jnp.bfloat16),
            pltpu.VMEM((HW, window_count, samples), jnp.bfloat16),
            buffers(),
            buffers(),
            buffers(),
            pltpu.VMEM((ROUNDS, bins, channel_count, 2 * channel_count), jnp.float32),
            pltpu.SemaphoreType.DMA((2,)),
            pltpu.SemaphoreType.DMA((2,)),
            pltpu.SemaphoreType.DMA((parts, chunks)),
            pltpu.SemaphoreType.DMA((parts, chunks)),
            pltpu.SemaphoreType.DMA((parts, chunks)),
            pltpu.SemaphoreType.DMA((parts, chunks)),
        ],
        compiler_params=pltpu.CompilerParams(
            collective_id=0, has_side_effects=True, vmem_limit_bytes=63 * 1024 * 1024
        ),
    )(traces, *consts)


def solution(mesh):
    placed = (P("blk", None, None), P())
    return jax.shard_map(
        per_device,
        mesh=mesh,
        in_specs=placed,
        out_specs=P("blk", None, None, None, None),
        check_vma=False,
    )
```

```python
import functools
import math

import jax
import jax.numpy as jnp
from jax import lax
from jax.experimental import pallas as pl
from jax.experimental.pallas import tpu as pltpu
from jax.sharding import PartitionSpec as P

MESH = pl.DeviceIdType.MESH

HW = 16
RAM_HALF = 64
ROUNDS = 2


epsilon = 1e-05
floor_power = 0.25


def with_halo(cells, sides, width):
    for axis, dim in sides:
        count = lax.axis_size(axis)
        ends = count - 1
        head = lax.slice_in_dim(cells, 0, width, axis=dim)
        tail = lax.slice_in_dim(cells, cells.shape[dim] - width, cells.shape[dim], axis=dim)
        cells = jnp.concatenate(
            [
                lax.ppermute(tail, axis, [(i, (i + 1) % count) for i in range(ends)]),
                cells,
                lax.ppermute(head, axis, [((i + 1) % count, i) for i in range(ends)]),
            ],
            axis=dim,
        )
    return cells


def shifted(shard, axis, by):
    count = lax.axis_size(axis)
    return lax.ppermute(shard, axis, [(i, (i + by) % count) for i in range(count)])


def prepare(extended, first_channel, total_channels, bands, halo_width, ram_half):
    channel_count = extended.shape[0] - 2 * halo_width
    ext_rows = extended.shape[0]
    window_count = extended.shape[1]
    samples = extended.shape[2]
    bin_count = samples // 2
    inner = jnp.arange(channel_count, dtype=jnp.int32)
    outer = jnp.arange(ext_rows, dtype=jnp.int32)
    offset = outer[None, :] - inner[:, None]
    outer_position = first_channel - halo_width + outer
    inside = (outer_position >= 0) & (outer_position < total_channels)
    selector = (offset >= 0) & (offset <= 2 * halo_width) & inside[None, :]
    neighbour_count = jnp.sum(selector.astype(jnp.float32), axis=1)
    neighbour_sum = jnp.einsum(
        "ie,ewl->iwl", selector.astype(jnp.bfloat16), extended, preferred_element_type=jnp.float32
    )
    centred = (
        extended[halo_width : halo_width + channel_count].astype(jnp.float32)
        - neighbour_sum / neighbour_count[:, None, None]
    )
    balanced = centred.astype(jnp.bfloat16)
    magnitude = jnp.abs(balanced)
    sample_index = jnp.arange(samples, dtype=jnp.int32)
    ram_band = jnp.abs(sample_index[:, None] - sample_index[None, :]) <= ram_half
    ram_count = jnp.sum(ram_band.astype(jnp.float32), axis=0)
    ram_sum = jnp.einsum(
        "cwl,lm->cwm", magnitude, ram_band.astype(jnp.bfloat16), preferred_element_type=jnp.float32
    )
    envelope = ram_sum / ram_count + epsilon
    normalized = (balanced.astype(jnp.float32) / envelope).astype(jnp.bfloat16)
    frequency = jnp.arange(1, bin_count + 1, dtype=jnp.int32)
    phase_steps = frequency[:, None] * sample_index[None, :] % samples
    phase = 2.0 * math.pi / samples * phase_steps.astype(jnp.float32)
    dft_table = (
        jnp.concatenate([jnp.cos(phase), -jnp.sin(phase)], axis=0) / math.sqrt(samples)
    ).astype(jnp.bfloat16)
    spectra = jnp.einsum("jl,cwl->jwc", dft_table, normalized, preferred_element_type=jnp.float32)
    spectra = spectra.reshape(2, bin_count, window_count, channel_count)
    power_bins = spectra[0] * spectra[0] + spectra[1] * spectra[1]
    same_band = (bands[:, None] == bands[None, :]).astype(jnp.float32)
    band_matrix = same_band / jnp.sum(same_band, axis=1, keepdims=True)
    band_mean = jnp.einsum("fg,gwc->fwc", band_matrix, power_bins, precision=lax.Precision.HIGHEST)
    whiten_scale = lax.rsqrt(jnp.maximum(band_mean, floor_power))
    return (spectra * whiten_scale[None]).astype(jnp.bfloat16)


def whiten_block(block, sel, count, ram, ram_count, table, band):
    halo = (block.shape[0] - sel.shape[0]) // 2
    channels = sel.shape[0]
    bins = band.shape[0]
    block = jnp.swapaxes(block.astype(jnp.float32), 0, 1)
    rows = []
    for w in range(block.shape[0]):
        x = block[w]
        neighbour_sum = jnp.dot(sel, x.astype(jnp.bfloat16), preferred_element_type=jnp.float32)
        balanced = (x[halo : halo + channels] - neighbour_sum / count).astype(jnp.bfloat16)
        ram_sum = jnp.dot(jnp.abs(balanced), ram, preferred_element_type=jnp.float32)
        envelope = ram_sum / ram_count + epsilon
        normalized = (balanced.astype(jnp.float32) / envelope).astype(jnp.bfloat16)
        spectra = lax.dot_general(
            table, normalized, (((1,), (1,)), ((), ())), preferred_element_type=jnp.float32
        )
        real, imag = spectra[:bins], spectra[bins:]
        power = real * real + imag * imag
        band_mean = jnp.dot(band, power, precision=lax.Precision.HIGHEST, preferred_element_type=jnp.float32)
        scale = lax.rsqrt(jnp.maximum(band_mean, floor_power))
        rows.append(jnp.concatenate([real * scale, imag * scale], axis=0))
    whitened = jnp.swapaxes(jnp.stack(rows, axis=0), 0, 1)
    return whitened.reshape(2, bins, whitened.shape[1], channels)


def prepare_kernel(ext_ref, sel_ref, count_ref, ram_ref, ram_count_ref, table_ref, band_ref, out_ref):
    consts = [r[...] for r in (sel_ref, count_ref, ram_ref, ram_count_ref, table_ref, band_ref)]
    out_ref[...] = whiten_block(ext_ref[...], *consts).astype(out_ref.dtype)


def constants(first_channel, total_channels, bands, channel_count, halo_width, samples, ram_half):
    ext_rows = channel_count + 2 * halo_width
    bin_count = samples // 2
    inner = jnp.arange(channel_count, dtype=jnp.int32)
    outer = jnp.arange(ext_rows, dtype=jnp.int32)
    offset = outer[None, :] - inner[:, None]
    outer_position = first_channel - halo_width + outer
    inside = (outer_position >= 0) & (outer_position < total_channels)
    selector = (offset >= 0) & (offset <= 2 * halo_width) & inside[None, :]
    neighbour_count = jnp.sum(selector.astype(jnp.float32), axis=1)[:, None]
    sample_index = jnp.arange(samples, dtype=jnp.int32)
    ram_band = jnp.abs(sample_index[:, None] - sample_index[None, :]) <= ram_half
    ram_count = jnp.sum(ram_band.astype(jnp.float32), axis=0)[None, :]
    frequency = jnp.arange(1, bin_count + 1, dtype=jnp.int32)
    phase_steps = frequency[:, None] * sample_index[None, :] % samples
    phase = 2.0 * math.pi / samples * phase_steps.astype(jnp.float32)
    dft_table = (
        jnp.concatenate([jnp.cos(phase), -jnp.sin(phase)], axis=0) / math.sqrt(samples)
    ).astype(jnp.bfloat16)
    same_band = (bands[:, None] == bands[None, :]).astype(jnp.float32)
    band_matrix = same_band / jnp.sum(same_band, axis=1, keepdims=True)
    return [
        selector.astype(jnp.bfloat16),
        neighbour_count,
        ram_band.astype(jnp.bfloat16),
        ram_count,
        dft_table,
        band_matrix,
    ]


def prepare_fast(extended, consts, windows, step=16):
    ext_rows, _, samples = extended.shape
    channel_count = consts[0].shape[0]
    bin_count = samples // 2
    whole = lambda i: (0, 0)
    return pl.pallas_call(
        prepare_kernel,
        out_shape=jax.ShapeDtypeStruct((2, bin_count, windows, channel_count), jnp.bfloat16),
        grid=(windows // step,),
        in_specs=[pl.BlockSpec((ext_rows, step, samples), lambda i: (0, i, 0))]
        + [pl.BlockSpec(c.shape, whole) for c in consts],
        out_specs=pl.BlockSpec((2, bin_count, step, channel_count), lambda i: (0, 0, i, 0)),
    )(extended, *consts)


def correlate_chunk(own, partners, acc, out, rows, scale, mode):
    dims = (((0,), (0,)), ((), ()))
    width = own.shape[-1]
    pieces = [[[] for _ in range(2)] for _ in partners]
    for j in range(rows.size):
        f = rows.start + j
        x = own[:, f]
        lhs = x.reshape(-1, width)
        sides = []
        for partner in partners:
            y = partner[:, f]
            sides += [y.reshape(-1, width), jnp.concatenate([-y[1], y[0]], axis=0)]
        rhs = jnp.concatenate(sides, axis=1)
        both = lax.dot_general(lhs, rhs, dims, preferred_element_type=jnp.float32)
        if mode == "first":
            acc[f] = both
        elif mode == "middle":
            acc[f] = acc[f] + both
        else:
            total = acc[f] + both
            for r in range(len(partners)):
                for o in range(2):
                    k = 2 * r + o
                    pieces[r][o].append(total[:, k * width : (k + 1) * width] / scale)
    if mode == "last":
        for r in range(len(partners)):
            for o in range(2):
                out[:, r, o, rows, :] = jnp.stack(pieces[r][o], axis=1).astype(out.dtype)


def exchange_kernel(n, chunks, scale, step, bounds, traces, sel, count, ram, ram_count, table, band,
                    out, head, tail, owns, first, second, acc, halo_send, halo_recv,
                    first_send, first_recv, second_send, second_recv):
    me = lax.axis_index("blk")
    core = lax.rem(me, 2)
    down = lax.rem(me + n - 2, n)
    up = lax.rem(me + 2, n)
    left = lax.rem(me + n - 1, n)
    right = lax.rem(me + 1, n)
    mate = me + 1 - 2 * core
    halo = head.shape[0]
    channels = traces.shape[0]

    barrier = pltpu.get_barrier_semaphore()
    for peer in (down, up, left, right):
        pl.semaphore_signal(barrier, inc=1, device_id=(peer,), device_id_type=MESH)
    pl.semaphore_wait(barrier, 4)

    to_right = pltpu.make_async_remote_copy(
        traces.at[pl.ds(channels - halo, halo)], head, halo_send.at[0], halo_recv.at[0],
        device_id=(right,), device_id_type=MESH)
    to_left = pltpu.make_async_remote_copy(
        traces.at[pl.ds(0, halo)], tail, halo_send.at[1], halo_recv.at[1],
        device_id=(left,), device_id_type=MESH)
    to_right.start()
    to_left.start()

    size = owns[0].shape[1] // chunks

    def part(i):
        return pl.ds(pl.multiple_of(i * size, size), size)

    def to_down(p, i):
        return pltpu.make_async_remote_copy(
            owns[p].at[:, part(i)], second[p].at[:, part(i)], second_send.at[p, i], second_recv.at[p, i],
            device_id=(down,), device_id_type=MESH)

    def to_mate(src, p, i):
        return pltpu.make_async_remote_copy(
            src.at[:, part(i)], first[p].at[:, part(i)], first_send.at[p, i], first_recv.at[p, i],
            device_id=(mate,), device_id_type=MESH)

    def send_part(p):
        @pl.loop(0, chunks)
        def _(i):
            to_down(p, i).start()

        @pl.when(core == 1)
        def _():
            @pl.loop(0, chunks)
            def _(i):
                to_mate(owns[p], p, i).start()

    consts = [r[...] for r in (sel, count, ram, ram_count, table, band)]
    to_right.wait_recv()
    to_left.wait_recv()
    for p, (start, length) in enumerate(bounds):
        late = owns[p]

        @pl.loop(0, length // step)
        def _(b):
            src = pl.ds(pl.multiple_of(start + b * step, step), step)
            dst = pl.ds(pl.multiple_of(b * step, step), step)
            block = jnp.concatenate([head[:, src, :], traces[:, src, :], tail[:, src, :]], axis=0)
            late[:, :, dst, :] = whiten_block(block, *consts).astype(late.dtype)

        send_part(p)

    parts = len(owns)
    for p in range(parts):
        mode = "first" if p == 0 else ("last" if p == parts - 1 else "middle")

        @pl.loop(0, chunks)
        def _(i):
            to_down(p, i).wait_recv()

            @pl.when(core == 0)
            def _():
                to_mate(second[p], p, i).start()

            to_mate(second[p], p, i).wait_recv()
            correlate_chunk(owns[p], (first[p], second[p]), acc, out, part(i), scale, mode)

    to_right.wait_send()
    to_left.wait_send()

    @pl.loop(0, chunks)
    def _(i):
        for p in range(parts):
            to_down(p, i).wait_send()
            to_mate(second[p], p, i).wait_send()


def per_device(traces, bands, chunks=4, split=(16, 32, 48, 48), step=16):
    channel_count, window_count, samples = traces.shape
    n = lax.axis_size("blk")
    first_channel = lax.axis_index("blk") * channel_count
    consts = constants(first_channel, channel_count * n, bands, channel_count, HW, samples, RAM_HALF)
    bounds, start = [], 0
    for length in split:
        bounds.append((start, length))
        start += length
    bins = samples // 2
    shapes = [(2, bins, length, channel_count) for length in split]
    buffers = lambda: [pltpu.VMEM(shape, jnp.bfloat16) for shape in shapes]
    vmem = pl.BlockSpec(memory_space=pltpu.VMEM)
    parts = len(split)
    return pl.pallas_call(
        functools.partial(exchange_kernel, n, chunks, math.sqrt(window_count), step, bounds),
        out_shape=jax.ShapeDtypeStruct((channel_count, ROUNDS, 2, bins, channel_count), jnp.bfloat16),
        in_specs=[vmem] * 7,
        out_specs=vmem,
        scratch_shapes=[
            pltpu.VMEM((HW, window_count, samples), jnp.bfloat16),
            pltpu.VMEM((HW, window_count, samples), jnp.bfloat16),
            buffers(),
            buffers(),
            buffers(),
            pltpu.VMEM((bins, channel_count, 2 * ROUNDS * channel_count), jnp.float32),
            pltpu.SemaphoreType.DMA((2,)),
            pltpu.SemaphoreType.DMA((2,)),
            pltpu.SemaphoreType.DMA((parts, chunks)),
            pltpu.SemaphoreType.DMA((parts, chunks)),
            pltpu.SemaphoreType.DMA((parts, chunks)),
            pltpu.SemaphoreType.DMA((parts, chunks)),
        ],
        compiler_params=pltpu.CompilerParams(
            collective_id=0, has_side_effects=True, vmem_limit_bytes=63 * 1024 * 1024
        ),
    )(traces, *consts)


def solution(mesh):
    placed = (P("blk", None, None), P())
    return jax.shard_map(
        per_device,
        mesh=mesh,
        in_specs=placed,
        out_specs=P("blk", None, None, None, None),
        check_vma=False,
    )
```

```python
import functools
import math

import jax
import jax.numpy as jnp
from jax import lax
from jax.experimental import pallas as pl
from jax.experimental.pallas import tpu as pltpu
from jax.sharding import PartitionSpec as P

MESH = pl.DeviceIdType.MESH

HW = 16
RAM_HALF = 64
ROUNDS = 2


epsilon = 1e-05
floor_power = 0.25


def with_halo(cells, sides, width):
    for axis, dim in sides:
        count = lax.axis_size(axis)
        ends = count - 1
        head = lax.slice_in_dim(cells, 0, width, axis=dim)
        tail = lax.slice_in_dim(cells, cells.shape[dim] - width, cells.shape[dim], axis=dim)
        cells = jnp.concatenate(
            [
                lax.ppermute(tail, axis, [(i, (i + 1) % count) for i in range(ends)]),
                cells,
                lax.ppermute(head, axis, [((i + 1) % count, i) for i in range(ends)]),
            ],
            axis=dim,
        )
    return cells


def shifted(shard, axis, by):
    count = lax.axis_size(axis)
    return lax.ppermute(shard, axis, [(i, (i + by) % count) for i in range(count)])


def prepare(extended, first_channel, total_channels, bands, halo_width, ram_half):
    channel_count = extended.shape[0] - 2 * halo_width
    ext_rows = extended.shape[0]
    window_count = extended.shape[1]
    samples = extended.shape[2]
    bin_count = samples // 2
    inner = jnp.arange(channel_count, dtype=jnp.int32)
    outer = jnp.arange(ext_rows, dtype=jnp.int32)
    offset = outer[None, :] - inner[:, None]
    outer_position = first_channel - halo_width + outer
    inside = (outer_position >= 0) & (outer_position < total_channels)
    selector = (offset >= 0) & (offset <= 2 * halo_width) & inside[None, :]
    neighbour_count = jnp.sum(selector.astype(jnp.float32), axis=1)
    neighbour_sum = jnp.einsum(
        "ie,ewl->iwl", selector.astype(jnp.bfloat16), extended, preferred_element_type=jnp.float32
    )
    centred = (
        extended[halo_width : halo_width + channel_count].astype(jnp.float32)
        - neighbour_sum / neighbour_count[:, None, None]
    )
    balanced = centred.astype(jnp.bfloat16)
    magnitude = jnp.abs(balanced)
    sample_index = jnp.arange(samples, dtype=jnp.int32)
    ram_band = jnp.abs(sample_index[:, None] - sample_index[None, :]) <= ram_half
    ram_count = jnp.sum(ram_band.astype(jnp.float32), axis=0)
    ram_sum = jnp.einsum(
        "cwl,lm->cwm", magnitude, ram_band.astype(jnp.bfloat16), preferred_element_type=jnp.float32
    )
    envelope = ram_sum / ram_count + epsilon
    normalized = (balanced.astype(jnp.float32) / envelope).astype(jnp.bfloat16)
    frequency = jnp.arange(1, bin_count + 1, dtype=jnp.int32)
    phase_steps = frequency[:, None] * sample_index[None, :] % samples
    phase = 2.0 * math.pi / samples * phase_steps.astype(jnp.float32)
    dft_table = (
        jnp.concatenate([jnp.cos(phase), -jnp.sin(phase)], axis=0) / math.sqrt(samples)
    ).astype(jnp.bfloat16)
    spectra = jnp.einsum("jl,cwl->jwc", dft_table, normalized, preferred_element_type=jnp.float32)
    spectra = spectra.reshape(2, bin_count, window_count, channel_count)
    power_bins = spectra[0] * spectra[0] + spectra[1] * spectra[1]
    same_band = (bands[:, None] == bands[None, :]).astype(jnp.float32)
    band_matrix = same_band / jnp.sum(same_band, axis=1, keepdims=True)
    band_mean = jnp.einsum("fg,gwc->fwc", band_matrix, power_bins, precision=lax.Precision.HIGHEST)
    whiten_scale = lax.rsqrt(jnp.maximum(band_mean, floor_power))
    return (spectra * whiten_scale[None]).astype(jnp.bfloat16)


def whiten_block(block, sel, count, ram, ram_count, table, band):
    halo = (block.shape[0] - sel.shape[0]) // 2
    channels = sel.shape[0]
    bins = band.shape[0]
    block = jnp.swapaxes(block.astype(jnp.float32), 0, 1)
    rows = []
    for w in range(block.shape[0]):
        x = block[w]
        neighbour_sum = jnp.dot(sel, x.astype(jnp.bfloat16), preferred_element_type=jnp.float32)
        balanced = (x[halo : halo + channels] - neighbour_sum * count).astype(jnp.bfloat16)
        ram_sum = jnp.dot(jnp.abs(balanced), ram, preferred_element_type=jnp.float32)
        envelope = ram_sum * ram_count + epsilon
        normalized = (balanced.astype(jnp.float32) / envelope).astype(jnp.bfloat16)
        spectra = lax.dot_general(
            table, normalized, (((1,), (1,)), ((), ())), preferred_element_type=jnp.float32
        )
        real, imag = spectra[:bins], spectra[bins:]
        power = real * real + imag * imag
        band_mean = jnp.dot(band, power, precision=lax.Precision.HIGHEST, preferred_element_type=jnp.float32)
        scale = lax.rsqrt(jnp.maximum(band_mean, floor_power))
        rows.append(jnp.concatenate([real * scale, imag * scale], axis=0))
    whitened = jnp.swapaxes(jnp.stack(rows, axis=0), 0, 1)
    return whitened.reshape(2, bins, whitened.shape[1], channels)


def prepare_kernel(ext_ref, sel_ref, count_ref, ram_ref, ram_count_ref, table_ref, band_ref, out_ref):
    consts = [r[...] for r in (sel_ref, count_ref, ram_ref, ram_count_ref, table_ref, band_ref)]
    out_ref[...] = whiten_block(ext_ref[...], *consts).astype(out_ref.dtype)


def constants(first_channel, total_channels, bands, channel_count, halo_width, samples, ram_half):
    ext_rows = channel_count + 2 * halo_width
    bin_count = samples // 2
    inner = jnp.arange(channel_count, dtype=jnp.int32)
    outer = jnp.arange(ext_rows, dtype=jnp.int32)
    offset = outer[None, :] - inner[:, None]
    outer_position = first_channel - halo_width + outer
    inside = (outer_position >= 0) & (outer_position < total_channels)
    selector = (offset >= 0) & (offset <= 2 * halo_width) & inside[None, :]
    neighbour_count = jnp.sum(selector.astype(jnp.float32), axis=1)[:, None]
    sample_index = jnp.arange(samples, dtype=jnp.int32)
    ram_band = jnp.abs(sample_index[:, None] - sample_index[None, :]) <= ram_half
    ram_count = jnp.sum(ram_band.astype(jnp.float32), axis=0)[None, :]
    frequency = jnp.arange(1, bin_count + 1, dtype=jnp.int32)
    phase_steps = frequency[:, None] * sample_index[None, :] % samples
    phase = 2.0 * math.pi / samples * phase_steps.astype(jnp.float32)
    dft_table = (
        jnp.concatenate([jnp.cos(phase), -jnp.sin(phase)], axis=0) / math.sqrt(samples)
    ).astype(jnp.bfloat16)
    same_band = (bands[:, None] == bands[None, :]).astype(jnp.float32)
    band_matrix = same_band / jnp.sum(same_band, axis=1, keepdims=True)
    return [
        selector.astype(jnp.bfloat16),
        1.0 / neighbour_count,
        ram_band.astype(jnp.bfloat16),
        1.0 / ram_count,
        dft_table,
        band_matrix,
    ]


def prepare_fast(extended, consts, windows, step=16):
    ext_rows, _, samples = extended.shape
    channel_count = consts[0].shape[0]
    bin_count = samples // 2
    whole = lambda i: (0, 0)
    return pl.pallas_call(
        prepare_kernel,
        out_shape=jax.ShapeDtypeStruct((2, bin_count, windows, channel_count), jnp.bfloat16),
        grid=(windows // step,),
        in_specs=[pl.BlockSpec((ext_rows, step, samples), lambda i: (0, i, 0))]
        + [pl.BlockSpec(c.shape, whole) for c in consts],
        out_specs=pl.BlockSpec((2, bin_count, step, channel_count), lambda i: (0, 0, i, 0)),
    )(extended, *consts)


def correlate_chunk(own, partners, acc, out, rows, scale, mode):
    dims = (((0,), (0,)), ((), ()))
    width = own.shape[-1]
    pieces = [[[] for _ in range(2)] for _ in partners]
    for j in range(rows.size):
        f = rows.start + j
        x = own[:, f]
        lhs = x.reshape(-1, width)
        sides = []
        for partner in partners:
            y = partner[:, f]
            sides += [y.reshape(-1, width), jnp.concatenate([-y[1], y[0]], axis=0)]
        rhs = jnp.concatenate(sides, axis=1)
        both = lax.dot_general(lhs, rhs, dims, preferred_element_type=jnp.float32)
        if mode == "first":
            acc[f] = both
        elif mode == "middle":
            acc[f] = acc[f] + both
        else:
            total = acc[f] + both
            for r in range(len(partners)):
                for o in range(2):
                    k = 2 * r + o
                    pieces[r][o].append(total[:, k * width : (k + 1) * width] / scale)
    if mode == "last":
        for r in range(len(partners)):
            for o in range(2):
                out[:, r, o, rows, :] = jnp.stack(pieces[r][o], axis=1).astype(out.dtype)


def exchange_kernel(n, chunks, scale, step, bounds, traces, sel, count, ram, ram_count, table, band,
                    out, head, tail, owns, first, second, acc, halo_send, halo_recv,
                    first_send, first_recv, second_send, second_recv):
    me = lax.axis_index("blk")
    core = lax.rem(me, 2)
    down = lax.rem(me + n - 2, n)
    up = lax.rem(me + 2, n)
    left = lax.rem(me + n - 1, n)
    right = lax.rem(me + 1, n)
    mate = me + 1 - 2 * core
    halo = head.shape[0]
    channels = traces.shape[0]

    barrier = pltpu.get_barrier_semaphore()
    for peer in (down, up, left, right):
        pl.semaphore_signal(barrier, inc=1, device_id=(peer,), device_id_type=MESH)
    pl.semaphore_wait(barrier, 4)

    to_right = pltpu.make_async_remote_copy(
        traces.at[pl.ds(channels - halo, halo)], head, halo_send.at[0], halo_recv.at[0],
        device_id=(right,), device_id_type=MESH)
    to_left = pltpu.make_async_remote_copy(
        traces.at[pl.ds(0, halo)], tail, halo_send.at[1], halo_recv.at[1],
        device_id=(left,), device_id_type=MESH)
    to_right.start()
    to_left.start()

    size = owns[0].shape[1] // chunks

    def part(i):
        return pl.ds(pl.multiple_of(i * size, size), size)

    def to_down(p, i):
        return pltpu.make_async_remote_copy(
            owns[p].at[:, part(i)], second[p].at[:, part(i)], second_send.at[p, i], second_recv.at[p, i],
            device_id=(down,), device_id_type=MESH)

    def to_mate(src, p, i):
        return pltpu.make_async_remote_copy(
            src.at[:, part(i)], first[p].at[:, part(i)], first_send.at[p, i], first_recv.at[p, i],
            device_id=(mate,), device_id_type=MESH)

    def send_part(p):
        @pl.loop(0, chunks)
        def _(i):
            to_down(p, i).start()

        @pl.when(core == 1)
        def _():
            @pl.loop(0, chunks)
            def _(i):
                to_mate(owns[p], p, i).start()

    consts = [r[...] for r in (sel, count, ram, ram_count, table, band)]
    to_right.wait_recv()
    to_left.wait_recv()
    for p, (start, length) in enumerate(bounds):
        late = owns[p]

        @pl.loop(0, length // step)
        def _(b):
            src = pl.ds(pl.multiple_of(start + b * step, step), step)
            dst = pl.ds(pl.multiple_of(b * step, step), step)
            block = jnp.concatenate([head[:, src, :], traces[:, src, :], tail[:, src, :]], axis=0)
            late[:, :, dst, :] = whiten_block(block, *consts).astype(late.dtype)

        send_part(p)

    parts = len(owns)
    for p in range(parts):
        mode = "first" if p == 0 else ("last" if p == parts - 1 else "middle")

        @pl.loop(0, chunks)
        def _(i):
            to_down(p, i).wait_recv()

            @pl.when(core == 0)
            def _():
                to_mate(second[p], p, i).start()

            to_mate(second[p], p, i).wait_recv()
            correlate_chunk(owns[p], (first[p], second[p]), acc, out, part(i), scale, mode)

    to_right.wait_send()
    to_left.wait_send()

    @pl.loop(0, chunks)
    def _(i):
        for p in range(parts):
            to_down(p, i).wait_send()
            to_mate(second[p], p, i).wait_send()


def per_device(traces, bands, chunks=4, split=(16, 32, 48, 48), step=16):
    channel_count, window_count, samples = traces.shape
    n = lax.axis_size("blk")
    first_channel = lax.axis_index("blk") * channel_count
    consts = constants(first_channel, channel_count * n, bands, channel_count, HW, samples, RAM_HALF)
    bounds, start = [], 0
    for length in split:
        bounds.append((start, length))
        start += length
    bins = samples // 2
    shapes = [(2, bins, length, channel_count) for length in split]
    buffers = lambda: [pltpu.VMEM(shape, jnp.bfloat16) for shape in shapes]
    vmem = pl.BlockSpec(memory_space=pltpu.VMEM)
    parts = len(split)
    return pl.pallas_call(
        functools.partial(exchange_kernel, n, chunks, math.sqrt(window_count), step, bounds),
        out_shape=jax.ShapeDtypeStruct((channel_count, ROUNDS, 2, bins, channel_count), jnp.bfloat16),
        in_specs=[vmem] * 7,
        out_specs=vmem,
        scratch_shapes=[
            pltpu.VMEM((HW, window_count, samples), jnp.bfloat16),
            pltpu.VMEM((HW, window_count, samples), jnp.bfloat16),
            buffers(),
            buffers(),
            buffers(),
            pltpu.VMEM((bins, channel_count, 2 * ROUNDS * channel_count), jnp.float32),
            pltpu.SemaphoreType.DMA((2,)),
            pltpu.SemaphoreType.DMA((2,)),
            pltpu.SemaphoreType.DMA((parts, chunks)),
            pltpu.SemaphoreType.DMA((parts, chunks)),
            pltpu.SemaphoreType.DMA((parts, chunks)),
            pltpu.SemaphoreType.DMA((parts, chunks)),
        ],
        compiler_params=pltpu.CompilerParams(
            collective_id=0, has_side_effects=True, vmem_limit_bytes=63 * 1024 * 1024
        ),
    )(traces, *consts)


def solution(mesh):
    placed = (P("blk", None, None), P())
    return jax.shard_map(
        per_device,
        mesh=mesh,
        in_specs=placed,
        out_specs=P("blk", None, None, None, None),
        check_vma=False,
    )
```

```python
import functools
import math

import jax
import jax.numpy as jnp
from jax import lax
from jax.experimental import pallas as pl
from jax.experimental.pallas import tpu as pltpu
from jax.sharding import PartitionSpec as P

MESH = pl.DeviceIdType.MESH

HW = 16
RAM_HALF = 64
ROUNDS = 2


epsilon = 1e-05
floor_power = 0.25


def with_halo(cells, sides, width):
    for axis, dim in sides:
        count = lax.axis_size(axis)
        ends = count - 1
        head = lax.slice_in_dim(cells, 0, width, axis=dim)
        tail = lax.slice_in_dim(cells, cells.shape[dim] - width, cells.shape[dim], axis=dim)
        cells = jnp.concatenate(
            [
                lax.ppermute(tail, axis, [(i, (i + 1) % count) for i in range(ends)]),
                cells,
                lax.ppermute(head, axis, [((i + 1) % count, i) for i in range(ends)]),
            ],
            axis=dim,
        )
    return cells


def shifted(shard, axis, by):
    count = lax.axis_size(axis)
    return lax.ppermute(shard, axis, [(i, (i + by) % count) for i in range(count)])


def prepare(extended, first_channel, total_channels, bands, halo_width, ram_half):
    channel_count = extended.shape[0] - 2 * halo_width
    ext_rows = extended.shape[0]
    window_count = extended.shape[1]
    samples = extended.shape[2]
    bin_count = samples // 2
    inner = jnp.arange(channel_count, dtype=jnp.int32)
    outer = jnp.arange(ext_rows, dtype=jnp.int32)
    offset = outer[None, :] - inner[:, None]
    outer_position = first_channel - halo_width + outer
    inside = (outer_position >= 0) & (outer_position < total_channels)
    selector = (offset >= 0) & (offset <= 2 * halo_width) & inside[None, :]
    neighbour_count = jnp.sum(selector.astype(jnp.float32), axis=1)
    neighbour_sum = jnp.einsum(
        "ie,ewl->iwl", selector.astype(jnp.bfloat16), extended, preferred_element_type=jnp.float32
    )
    centred = (
        extended[halo_width : halo_width + channel_count].astype(jnp.float32)
        - neighbour_sum / neighbour_count[:, None, None]
    )
    balanced = centred.astype(jnp.bfloat16)
    magnitude = jnp.abs(balanced)
    sample_index = jnp.arange(samples, dtype=jnp.int32)
    ram_band = jnp.abs(sample_index[:, None] - sample_index[None, :]) <= ram_half
    ram_count = jnp.sum(ram_band.astype(jnp.float32), axis=0)
    ram_sum = jnp.einsum(
        "cwl,lm->cwm", magnitude, ram_band.astype(jnp.bfloat16), preferred_element_type=jnp.float32
    )
    envelope = ram_sum / ram_count + epsilon
    normalized = (balanced.astype(jnp.float32) / envelope).astype(jnp.bfloat16)
    frequency = jnp.arange(1, bin_count + 1, dtype=jnp.int32)
    phase_steps = frequency[:, None] * sample_index[None, :] % samples
    phase = 2.0 * math.pi / samples * phase_steps.astype(jnp.float32)
    dft_table = (
        jnp.concatenate([jnp.cos(phase), -jnp.sin(phase)], axis=0) / math.sqrt(samples)
    ).astype(jnp.bfloat16)
    spectra = jnp.einsum("jl,cwl->jwc", dft_table, normalized, preferred_element_type=jnp.float32)
    spectra = spectra.reshape(2, bin_count, window_count, channel_count)
    power_bins = spectra[0] * spectra[0] + spectra[1] * spectra[1]
    same_band = (bands[:, None] == bands[None, :]).astype(jnp.float32)
    band_matrix = same_band / jnp.sum(same_band, axis=1, keepdims=True)
    band_mean = jnp.einsum("fg,gwc->fwc", band_matrix, power_bins, precision=lax.Precision.HIGHEST)
    whiten_scale = lax.rsqrt(jnp.maximum(band_mean, floor_power))
    return (spectra * whiten_scale[None]).astype(jnp.bfloat16)


def whiten_block(block, sel, count, ram, ram_count, table, band):
    halo = (block.shape[0] - sel.shape[0]) // 2
    channels = sel.shape[0]
    bins = band.shape[0]
    block = jnp.swapaxes(block.astype(jnp.float32), 0, 1)
    rows = []
    for w in range(block.shape[0]):
        x = block[w]
        neighbour_sum = jnp.dot(sel, x.astype(jnp.bfloat16), preferred_element_type=jnp.float32)
        balanced = (x[halo : halo + channels] - neighbour_sum / count).astype(jnp.bfloat16)
        ram_sum = jnp.dot(jnp.abs(balanced), ram, preferred_element_type=jnp.float32)
        envelope = ram_sum / ram_count + epsilon
        normalized = (balanced.astype(jnp.float32) / envelope).astype(jnp.bfloat16)
        spectra = lax.dot_general(
            table, normalized, (((1,), (1,)), ((), ())), preferred_element_type=jnp.float32
        )
        real, imag = spectra[:bins], spectra[bins:]
        power = real * real + imag * imag
        band_mean = jnp.dot(band, power, precision=lax.Precision.HIGHEST, preferred_element_type=jnp.float32)
        scale = lax.rsqrt(jnp.maximum(band_mean, floor_power))
        rows.append(jnp.concatenate([real * scale, imag * scale], axis=0))
    whitened = jnp.swapaxes(jnp.stack(rows, axis=0), 0, 1)
    return whitened.reshape(2, bins, whitened.shape[1], channels)


def prepare_kernel(ext_ref, sel_ref, count_ref, ram_ref, ram_count_ref, table_ref, band_ref, out_ref):
    consts = [r[...] for r in (sel_ref, count_ref, ram_ref, ram_count_ref, table_ref, band_ref)]
    out_ref[...] = whiten_block(ext_ref[...], *consts).astype(out_ref.dtype)


def constants(first_channel, total_channels, bands, channel_count, halo_width, samples, ram_half):
    ext_rows = channel_count + 2 * halo_width
    bin_count = samples // 2
    inner = jnp.arange(channel_count, dtype=jnp.int32)
    outer = jnp.arange(ext_rows, dtype=jnp.int32)
    offset = outer[None, :] - inner[:, None]
    outer_position = first_channel - halo_width + outer
    inside = (outer_position >= 0) & (outer_position < total_channels)
    selector = (offset >= 0) & (offset <= 2 * halo_width) & inside[None, :]
    neighbour_count = jnp.sum(selector.astype(jnp.float32), axis=1)[:, None]
    sample_index = jnp.arange(samples, dtype=jnp.int32)
    ram_band = jnp.abs(sample_index[:, None] - sample_index[None, :]) <= ram_half
    ram_count = jnp.sum(ram_band.astype(jnp.float32), axis=0)[None, :]
    frequency = jnp.arange(1, bin_count + 1, dtype=jnp.int32)
    phase_steps = frequency[:, None] * sample_index[None, :] % samples
    phase = 2.0 * math.pi / samples * phase_steps.astype(jnp.float32)
    dft_table = (
        jnp.concatenate([jnp.cos(phase), -jnp.sin(phase)], axis=0) / math.sqrt(samples)
    ).astype(jnp.bfloat16)
    same_band = (bands[:, None] == bands[None, :]).astype(jnp.float32)
    band_matrix = same_band / jnp.sum(same_band, axis=1, keepdims=True)
    return [
        selector.astype(jnp.bfloat16),
        neighbour_count,
        ram_band.astype(jnp.bfloat16),
        ram_count,
        dft_table,
        band_matrix,
    ]


def prepare_fast(extended, consts, windows, step=16):
    ext_rows, _, samples = extended.shape
    channel_count = consts[0].shape[0]
    bin_count = samples // 2
    whole = lambda i: (0, 0)
    return pl.pallas_call(
        prepare_kernel,
        out_shape=jax.ShapeDtypeStruct((2, bin_count, windows, channel_count), jnp.bfloat16),
        grid=(windows // step,),
        in_specs=[pl.BlockSpec((ext_rows, step, samples), lambda i: (0, i, 0))]
        + [pl.BlockSpec(c.shape, whole) for c in consts],
        out_specs=pl.BlockSpec((2, bin_count, step, channel_count), lambda i: (0, 0, i, 0)),
    )(extended, *consts)


def correlate_chunk(own, partner, acc, out, r, rows, scale, mode):
    dims = (((0,), (0,)), ((), ()))
    width = own.shape[-1]
    real_rows, imag_rows = [], []
    for j in range(rows.size):
        f = rows.start + j
        x = own[:, f]
        y = partner[:, f]
        lhs = x.reshape(-1, x.shape[-1])
        real_rhs = y.reshape(-1, y.shape[-1])
        imag_rhs = jnp.concatenate([-y[1], y[0]], axis=0)
        rhs = jnp.concatenate([real_rhs, imag_rhs], axis=1)
        both = lax.dot_general(lhs, rhs, dims, preferred_element_type=jnp.float32)
        if mode == "first":
            acc[r, f] = both
        elif mode == "middle":
            acc[r, f] = acc[r, f] + both
        else:
            total = acc[r, f] + both
            real_rows.append(total[:, :width] / scale)
            imag_rows.append(total[:, width:] / scale)
    if mode == "last":
        out[:, r, 0, rows, :] = jnp.stack(real_rows, axis=1).astype(out.dtype)
        out[:, r, 1, rows, :] = jnp.stack(imag_rows, axis=1).astype(out.dtype)


def exchange_kernel(n, chunks, scale, step, bounds, traces, sel, count, ram, ram_count, table, band,
                    out, head, tail, owns, first, second, acc, halo_send, halo_recv,
                    first_send, first_recv, second_send, second_recv):
    me = lax.axis_index("blk")
    core = lax.rem(me, 2)
    down = lax.rem(me + n - 2, n)
    up = lax.rem(me + 2, n)
    left = lax.rem(me + n - 1, n)
    right = lax.rem(me + 1, n)
    mate = me + 1 - 2 * core
    halo = head.shape[0]
    channels = traces.shape[0]

    barrier = pltpu.get_barrier_semaphore()
    for peer in (down, up, left, right):
        pl.semaphore_signal(barrier, inc=1, device_id=(peer,), device_id_type=MESH)
    pl.semaphore_wait(barrier, 4)

    to_right = pltpu.make_async_remote_copy(
        traces.at[pl.ds(channels - halo, halo)], head, halo_send.at[0], halo_recv.at[0],
        device_id=(right,), device_id_type=MESH)
    to_left = pltpu.make_async_remote_copy(
        traces.at[pl.ds(0, halo)], tail, halo_send.at[1], halo_recv.at[1],
        device_id=(left,), device_id_type=MESH)
    to_right.start()
    to_left.start()

    size = owns[0].shape[1] // chunks

    def part(i):
        return pl.ds(pl.multiple_of(i * size, size), size)

    def to_down(p, i):
        return pltpu.make_async_remote_copy(
            owns[p].at[:, part(i)], second[p].at[:, part(i)], second_send.at[p, i], second_recv.at[p, i],
            device_id=(down,), device_id_type=MESH)

    def to_mate(src, p, i):
        return pltpu.make_async_remote_copy(
            src.at[:, part(i)], first[p].at[:, part(i)], first_send.at[p, i], first_recv.at[p, i],
            device_id=(mate,), device_id_type=MESH)

    def send_part(p):
        @pl.loop(0, chunks)
        def _(i):
            to_down(p, i).start()

        @pl.when(core == 1)
        def _():
            @pl.loop(0, chunks)
            def _(i):
                to_mate(owns[p], p, i).start()

    consts = [r[...] for r in (sel, count, ram, ram_count, table, band)]
    to_right.wait_recv()
    to_left.wait_recv()
    for p, (start, length) in enumerate(bounds):
        late = owns[p]

        @pl.loop(0, length // step)
        def _(b):
            src = pl.ds(pl.multiple_of(start + b * step, step), step)
            dst = pl.ds(pl.multiple_of(b * step, step), step)
            block = jnp.concatenate([head[:, src, :], traces[:, src, :], tail[:, src, :]], axis=0)
            late[:, :, dst, :] = whiten_block(block, *consts).astype(late.dtype)

        send_part(p)

    parts = len(owns)
    for p in range(parts):
        mode = "first" if p == 0 else ("last" if p == parts - 1 else "middle")

        @pl.loop(0, chunks)
        def _(i):
            to_down(p, i).wait_recv()

            @pl.when(core == 0)
            def _():
                to_mate(second[p], p, i).start()

            correlate_chunk(owns[p], second[p], acc, out, 1, part(i), scale, mode)
            to_mate(second[p], p, i).wait_recv()
            correlate_chunk(owns[p], first[p], acc, out, 0, part(i), scale, mode)

    to_right.wait_send()
    to_left.wait_send()

    @pl.loop(0, chunks)
    def _(i):
        for p in range(parts):
            to_down(p, i).wait_send()
            to_mate(second[p], p, i).wait_send()


def per_device(traces, bands, chunks=2, split=(16, 32, 48, 48), step=16):
    channel_count, window_count, samples = traces.shape
    n = lax.axis_size("blk")
    first_channel = lax.axis_index("blk") * channel_count
    consts = constants(first_channel, channel_count * n, bands, channel_count, HW, samples, RAM_HALF)
    bounds, start = [], 0
    for length in split:
        bounds.append((start, length))
        start += length
    bins = samples // 2
    shapes = [(2, bins, length, channel_count) for length in split]
    buffers = lambda: [pltpu.VMEM(shape, jnp.bfloat16) for shape in shapes]
    vmem = pl.BlockSpec(memory_space=pltpu.VMEM)
    parts = len(split)
    return pl.pallas_call(
        functools.partial(exchange_kernel, n, chunks, math.sqrt(window_count), step, bounds),
        out_shape=jax.ShapeDtypeStruct((channel_count, ROUNDS, 2, bins, channel_count), jnp.bfloat16),
        in_specs=[vmem] * 7,
        out_specs=vmem,
        scratch_shapes=[
            pltpu.VMEM((HW, window_count, samples), jnp.bfloat16),
            pltpu.VMEM((HW, window_count, samples), jnp.bfloat16),
            buffers(),
            buffers(),
            buffers(),
            pltpu.VMEM((ROUNDS, bins, channel_count, 2 * channel_count), jnp.float32),
            pltpu.SemaphoreType.DMA((2,)),
            pltpu.SemaphoreType.DMA((2,)),
            pltpu.SemaphoreType.DMA((parts, chunks)),
            pltpu.SemaphoreType.DMA((parts, chunks)),
            pltpu.SemaphoreType.DMA((parts, chunks)),
            pltpu.SemaphoreType.DMA((parts, chunks)),
        ],
        compiler_params=pltpu.CompilerParams(
            collective_id=0, has_side_effects=True, vmem_limit_bytes=63 * 1024 * 1024
        ),
    )(traces, *consts)


def solution(mesh):
    placed = (P("blk", None, None), P())
    return jax.shard_map(
        per_device,
        mesh=mesh,
        in_specs=placed,
        out_specs=P("blk", None, None, None, None),
        check_vma=False,
    )
```

```python
import functools
import math

import ml_dtypes
import numpy as np

import jax
import jax.numpy as jnp
from jax import lax
from jax.experimental import pallas as pl
from jax.experimental.pallas import tpu as pltpu
from jax.sharding import PartitionSpec as P

MESH = pl.DeviceIdType.MESH

HW = 16
RAM_HALF = 64
ROUNDS = 2


epsilon = 1e-05
floor_power = 0.25


def with_halo(cells, sides, width):
    for axis, dim in sides:
        count = lax.axis_size(axis)
        ends = count - 1
        head = lax.slice_in_dim(cells, 0, width, axis=dim)
        tail = lax.slice_in_dim(cells, cells.shape[dim] - width, cells.shape[dim], axis=dim)
        cells = jnp.concatenate(
            [
                lax.ppermute(tail, axis, [(i, (i + 1) % count) for i in range(ends)]),
                cells,
                lax.ppermute(head, axis, [((i + 1) % count, i) for i in range(ends)]),
            ],
            axis=dim,
        )
    return cells


def shifted(shard, axis, by):
    count = lax.axis_size(axis)
    return lax.ppermute(shard, axis, [(i, (i + by) % count) for i in range(count)])


def prepare(extended, first_channel, total_channels, bands, halo_width, ram_half):
    channel_count = extended.shape[0] - 2 * halo_width
    ext_rows = extended.shape[0]
    window_count = extended.shape[1]
    samples = extended.shape[2]
    bin_count = samples // 2
    inner = jnp.arange(channel_count, dtype=jnp.int32)
    outer = jnp.arange(ext_rows, dtype=jnp.int32)
    offset = outer[None, :] - inner[:, None]
    outer_position = first_channel - halo_width + outer
    inside = (outer_position >= 0) & (outer_position < total_channels)
    selector = (offset >= 0) & (offset <= 2 * halo_width) & inside[None, :]
    neighbour_count = jnp.sum(selector.astype(jnp.float32), axis=1)
    neighbour_sum = jnp.einsum(
        "ie,ewl->iwl", selector.astype(jnp.bfloat16), extended, preferred_element_type=jnp.float32
    )
    centred = (
        extended[halo_width : halo_width + channel_count].astype(jnp.float32)
        - neighbour_sum / neighbour_count[:, None, None]
    )
    balanced = centred.astype(jnp.bfloat16)
    magnitude = jnp.abs(balanced)
    sample_index = jnp.arange(samples, dtype=jnp.int32)
    ram_band = jnp.abs(sample_index[:, None] - sample_index[None, :]) <= ram_half
    ram_count = jnp.sum(ram_band.astype(jnp.float32), axis=0)
    ram_sum = jnp.einsum(
        "cwl,lm->cwm", magnitude, ram_band.astype(jnp.bfloat16), preferred_element_type=jnp.float32
    )
    envelope = ram_sum / ram_count + epsilon
    normalized = (balanced.astype(jnp.float32) / envelope).astype(jnp.bfloat16)
    frequency = jnp.arange(1, bin_count + 1, dtype=jnp.int32)
    phase_steps = frequency[:, None] * sample_index[None, :] % samples
    phase = 2.0 * math.pi / samples * phase_steps.astype(jnp.float32)
    dft_table = (
        jnp.concatenate([jnp.cos(phase), -jnp.sin(phase)], axis=0) / math.sqrt(samples)
    ).astype(jnp.bfloat16)
    spectra = jnp.einsum("jl,cwl->jwc", dft_table, normalized, preferred_element_type=jnp.float32)
    spectra = spectra.reshape(2, bin_count, window_count, channel_count)
    power_bins = spectra[0] * spectra[0] + spectra[1] * spectra[1]
    same_band = (bands[:, None] == bands[None, :]).astype(jnp.float32)
    band_matrix = same_band / jnp.sum(same_band, axis=1, keepdims=True)
    band_mean = jnp.einsum("fg,gwc->fwc", band_matrix, power_bins, precision=lax.Precision.HIGHEST)
    whiten_scale = lax.rsqrt(jnp.maximum(band_mean, floor_power))
    return (spectra * whiten_scale[None]).astype(jnp.bfloat16)


def whiten_block(block, sel, count, ram, ram_count, table, band):
    halo = (block.shape[0] - sel.shape[0]) // 2
    channels = sel.shape[0]
    bins = band.shape[0]
    block = jnp.swapaxes(block.astype(jnp.float32), 0, 1)
    rows = []
    for w in range(block.shape[0]):
        x = block[w]
        neighbour_sum = jnp.dot(sel, x.astype(jnp.bfloat16), preferred_element_type=jnp.float32)
        balanced = (x[halo : halo + channels] - neighbour_sum / count).astype(jnp.bfloat16)
        ram_sum = jnp.dot(jnp.abs(balanced), ram, preferred_element_type=jnp.float32)
        envelope = ram_sum / ram_count + epsilon
        normalized = (balanced.astype(jnp.float32) / envelope).astype(jnp.bfloat16)
        spectra = lax.dot_general(
            table, normalized, (((1,), (1,)), ((), ())), preferred_element_type=jnp.float32
        )
        real, imag = spectra[:bins], spectra[bins:]
        power = real * real + imag * imag
        band_mean = jnp.dot(band, power, precision=lax.Precision.HIGHEST, preferred_element_type=jnp.float32)
        scale = lax.rsqrt(jnp.maximum(band_mean, floor_power))
        rows.append(jnp.concatenate([real * scale, imag * scale], axis=0))
    whitened = jnp.swapaxes(jnp.stack(rows, axis=0), 0, 1)
    return whitened.reshape(2, bins, whitened.shape[1], channels)


def prepare_kernel(ext_ref, sel_ref, count_ref, ram_ref, ram_count_ref, table_ref, band_ref, out_ref):
    consts = [r[...] for r in (sel_ref, count_ref, ram_ref, ram_count_ref, table_ref, band_ref)]
    out_ref[...] = whiten_block(ext_ref[...], *consts).astype(out_ref.dtype)


def constants(first_channel, total_channels, bands, channel_count, halo_width, samples, ram_half):
    ext_rows = channel_count + 2 * halo_width
    bin_count = samples // 2
    inner = jnp.arange(channel_count, dtype=jnp.int32)
    outer = jnp.arange(ext_rows, dtype=jnp.int32)
    offset = outer[None, :] - inner[:, None]
    outer_position = first_channel - halo_width + outer
    inside = (outer_position >= 0) & (outer_position < total_channels)
    selector = (offset >= 0) & (offset <= 2 * halo_width) & inside[None, :]
    neighbour_count = jnp.sum(selector.astype(jnp.float32), axis=1)[:, None]
    sample_index = np.arange(samples, dtype=np.int32)
    ram_band = np.abs(sample_index[:, None] - sample_index[None, :]) <= ram_half
    ram_count = np.sum(ram_band.astype(np.float32), axis=0)[None, :]
    frequency = np.arange(1, bin_count + 1, dtype=np.int32)
    phase_steps = frequency[:, None] * sample_index[None, :] % samples
    phase = np.float32(2.0 * math.pi / samples) * phase_steps.astype(np.float32)
    dft_table = jnp.asarray(
        (np.concatenate([np.cos(phase), -np.sin(phase)], axis=0) / np.float32(math.sqrt(samples))).astype(
            ml_dtypes.bfloat16
        )
    )
    ram_count = jnp.asarray(ram_count)
    ram_band = jnp.asarray(ram_band)
    same_band = (bands[:, None] == bands[None, :]).astype(jnp.float32)
    band_matrix = same_band / jnp.sum(same_band, axis=1, keepdims=True)
    return [
        selector.astype(jnp.bfloat16),
        neighbour_count,
        ram_band.astype(jnp.bfloat16),
        ram_count,
        dft_table,
        band_matrix,
    ]


def prepare_fast(extended, consts, windows, step=16):
    ext_rows, _, samples = extended.shape
    channel_count = consts[0].shape[0]
    bin_count = samples // 2
    whole = lambda i: (0, 0)
    return pl.pallas_call(
        prepare_kernel,
        out_shape=jax.ShapeDtypeStruct((2, bin_count, windows, channel_count), jnp.bfloat16),
        grid=(windows // step,),
        in_specs=[pl.BlockSpec((ext_rows, step, samples), lambda i: (0, i, 0))]
        + [pl.BlockSpec(c.shape, whole) for c in consts],
        out_specs=pl.BlockSpec((2, bin_count, step, channel_count), lambda i: (0, 0, i, 0)),
    )(extended, *consts)


def correlate_chunk(own, partner, acc, out, r, rows, scale, mode):
    dims = (((0,), (0,)), ((), ()))
    width = own.shape[-1]
    real_rows, imag_rows = [], []
    for j in range(rows.size):
        f = rows.start + j
        x = own[:, f]
        y = partner[:, f]
        lhs = x.reshape(-1, x.shape[-1])
        real_rhs = y.reshape(-1, y.shape[-1])
        imag_rhs = jnp.concatenate([-y[1], y[0]], axis=0)
        rhs = jnp.concatenate([real_rhs, imag_rhs], axis=1)
        both = lax.dot_general(lhs, rhs, dims, preferred_element_type=jnp.float32)
        if mode == "first":
            acc[r, f] = both
        elif mode == "middle":
            acc[r, f] = acc[r, f] + both
        else:
            total = acc[r, f] + both
            real_rows.append(total[:, :width] / scale)
            imag_rows.append(total[:, width:] / scale)
    if mode == "last":
        out[:, r, 0, rows, :] = jnp.stack(real_rows, axis=1).astype(out.dtype)
        out[:, r, 1, rows, :] = jnp.stack(imag_rows, axis=1).astype(out.dtype)


def exchange_kernel(n, chunks, scale, step, bounds, traces, sel, count, ram, ram_count, table, band,
                    out, head, tail, owns, first, second, acc, halo_send, halo_recv,
                    first_send, first_recv, second_send, second_recv):
    me = lax.axis_index("blk")
    core = lax.rem(me, 2)
    down = lax.rem(me + n - 2, n)
    up = lax.rem(me + 2, n)
    left = lax.rem(me + n - 1, n)
    right = lax.rem(me + 1, n)
    mate = me + 1 - 2 * core
    halo = head.shape[0]
    channels = traces.shape[0]

    barrier = pltpu.get_barrier_semaphore()
    for peer in (down, up, left, right):
        pl.semaphore_signal(barrier, inc=1, device_id=(peer,), device_id_type=MESH)
    pl.semaphore_wait(barrier, 4)

    to_right = pltpu.make_async_remote_copy(
        traces.at[pl.ds(channels - halo, halo)], head, halo_send.at[0], halo_recv.at[0],
        device_id=(right,), device_id_type=MESH)
    to_left = pltpu.make_async_remote_copy(
        traces.at[pl.ds(0, halo)], tail, halo_send.at[1], halo_recv.at[1],
        device_id=(left,), device_id_type=MESH)
    to_right.start()
    to_left.start()

    size = owns[0].shape[1] // chunks

    def part(i):
        return pl.ds(pl.multiple_of(i * size, size), size)

    def to_down(p, i):
        return pltpu.make_async_remote_copy(
            owns[p].at[:, part(i)], second[p].at[:, part(i)], second_send.at[p, i], second_recv.at[p, i],
            device_id=(down,), device_id_type=MESH)

    def to_mate(src, p, i):
        return pltpu.make_async_remote_copy(
            src.at[:, part(i)], first[p].at[:, part(i)], first_send.at[p, i], first_recv.at[p, i],
            device_id=(mate,), device_id_type=MESH)

    def send_part(p):
        @pl.loop(0, chunks)
        def _(i):
            to_down(p, i).start()

        @pl.when(core == 1)
        def _():
            @pl.loop(0, chunks)
            def _(i):
                to_mate(owns[p], p, i).start()

    consts = [r[...] for r in (sel, count, ram, ram_count, table, band)]
    to_right.wait_recv()
    to_left.wait_recv()
    for p, (start, length) in enumerate(bounds):
        late = owns[p]

        @pl.loop(0, length // step)
        def _(b):
            src = pl.ds(pl.multiple_of(start + b * step, step), step)
            dst = pl.ds(pl.multiple_of(b * step, step), step)
            block = jnp.concatenate([head[:, src, :], traces[:, src, :], tail[:, src, :]], axis=0)
            late[:, :, dst, :] = whiten_block(block, *consts).astype(late.dtype)

        send_part(p)

    parts = len(owns)
    for p in range(parts):
        mode = "first" if p == 0 else ("last" if p == parts - 1 else "middle")

        @pl.loop(0, chunks)
        def _(i):
            to_down(p, i).wait_recv()

            @pl.when(core == 0)
            def _():
                to_mate(second[p], p, i).start()

            correlate_chunk(owns[p], second[p], acc, out, 1, part(i), scale, mode)
            to_mate(second[p], p, i).wait_recv()
            correlate_chunk(owns[p], first[p], acc, out, 0, part(i), scale, mode)

    to_right.wait_send()
    to_left.wait_send()

    @pl.loop(0, chunks)
    def _(i):
        for p in range(parts):
            to_down(p, i).wait_send()
            to_mate(second[p], p, i).wait_send()


def per_device(traces, bands, chunks=4, split=(16, 32, 48, 48), step=16):
    channel_count, window_count, samples = traces.shape
    n = lax.axis_size("blk")
    first_channel = lax.axis_index("blk") * channel_count
    consts = constants(first_channel, channel_count * n, bands, channel_count, HW, samples, RAM_HALF)
    bounds, start = [], 0
    for length in split:
        bounds.append((start, length))
        start += length
    bins = samples // 2
    shapes = [(2, bins, length, channel_count) for length in split]
    buffers = lambda: [pltpu.VMEM(shape, jnp.bfloat16) for shape in shapes]
    vmem = pl.BlockSpec(memory_space=pltpu.VMEM)
    parts = len(split)
    return pl.pallas_call(
        functools.partial(exchange_kernel, n, chunks, math.sqrt(window_count), step, bounds),
        out_shape=jax.ShapeDtypeStruct((channel_count, ROUNDS, 2, bins, channel_count), jnp.bfloat16),
        in_specs=[vmem] * 7,
        out_specs=vmem,
        scratch_shapes=[
            pltpu.VMEM((HW, window_count, samples), jnp.bfloat16),
            pltpu.VMEM((HW, window_count, samples), jnp.bfloat16),
            buffers(),
            buffers(),
            buffers(),
            pltpu.VMEM((ROUNDS, bins, channel_count, 2 * channel_count), jnp.float32),
            pltpu.SemaphoreType.DMA((2,)),
            pltpu.SemaphoreType.DMA((2,)),
            pltpu.SemaphoreType.DMA((parts, chunks)),
            pltpu.SemaphoreType.DMA((parts, chunks)),
            pltpu.SemaphoreType.DMA((parts, chunks)),
            pltpu.SemaphoreType.DMA((parts, chunks)),
        ],
        compiler_params=pltpu.CompilerParams(
            collective_id=0, has_side_effects=True, vmem_limit_bytes=63 * 1024 * 1024
        ),
    )(traces, *consts)


def solution(mesh):
    placed = (P("blk", None, None), P())
    return jax.shard_map(
        per_device,
        mesh=mesh,
        in_specs=placed,
        out_specs=P("blk", None, None, None, None),
        check_vma=False,
    )
```

```python
import functools
import math

import ml_dtypes
import numpy as np

import jax
import jax.numpy as jnp
from jax import lax
from jax.experimental import pallas as pl
from jax.experimental.pallas import tpu as pltpu
from jax.sharding import PartitionSpec as P

MESH = pl.DeviceIdType.MESH

HW = 16
RAM_HALF = 64
ROUNDS = 2


epsilon = 1e-05
floor_power = 0.25


def with_halo(cells, sides, width):
    for axis, dim in sides:
        count = lax.axis_size(axis)
        ends = count - 1
        head = lax.slice_in_dim(cells, 0, width, axis=dim)
        tail = lax.slice_in_dim(cells, cells.shape[dim] - width, cells.shape[dim], axis=dim)
        cells = jnp.concatenate(
            [
                lax.ppermute(tail, axis, [(i, (i + 1) % count) for i in range(ends)]),
                cells,
                lax.ppermute(head, axis, [((i + 1) % count, i) for i in range(ends)]),
            ],
            axis=dim,
        )
    return cells


def shifted(shard, axis, by):
    count = lax.axis_size(axis)
    return lax.ppermute(shard, axis, [(i, (i + by) % count) for i in range(count)])


def prepare(extended, first_channel, total_channels, bands, halo_width, ram_half):
    channel_count = extended.shape[0] - 2 * halo_width
    ext_rows = extended.shape[0]
    window_count = extended.shape[1]
    samples = extended.shape[2]
    bin_count = samples // 2
    inner = jnp.arange(channel_count, dtype=jnp.int32)
    outer = jnp.arange(ext_rows, dtype=jnp.int32)
    offset = outer[None, :] - inner[:, None]
    outer_position = first_channel - halo_width + outer
    inside = (outer_position >= 0) & (outer_position < total_channels)
    selector = (offset >= 0) & (offset <= 2 * halo_width) & inside[None, :]
    neighbour_count = jnp.sum(selector.astype(jnp.float32), axis=1)
    neighbour_sum = jnp.einsum(
        "ie,ewl->iwl", selector.astype(jnp.bfloat16), extended, preferred_element_type=jnp.float32
    )
    centred = (
        extended[halo_width : halo_width + channel_count].astype(jnp.float32)
        - neighbour_sum / neighbour_count[:, None, None]
    )
    balanced = centred.astype(jnp.bfloat16)
    magnitude = jnp.abs(balanced)
    sample_index = jnp.arange(samples, dtype=jnp.int32)
    ram_band = jnp.abs(sample_index[:, None] - sample_index[None, :]) <= ram_half
    ram_count = jnp.sum(ram_band.astype(jnp.float32), axis=0)
    ram_sum = jnp.einsum(
        "cwl,lm->cwm", magnitude, ram_band.astype(jnp.bfloat16), preferred_element_type=jnp.float32
    )
    envelope = ram_sum / ram_count + epsilon
    normalized = (balanced.astype(jnp.float32) / envelope).astype(jnp.bfloat16)
    frequency = jnp.arange(1, bin_count + 1, dtype=jnp.int32)
    phase_steps = frequency[:, None] * sample_index[None, :] % samples
    phase = 2.0 * math.pi / samples * phase_steps.astype(jnp.float32)
    dft_table = (
        jnp.concatenate([jnp.cos(phase), -jnp.sin(phase)], axis=0) / math.sqrt(samples)
    ).astype(jnp.bfloat16)
    spectra = jnp.einsum("jl,cwl->jwc", dft_table, normalized, preferred_element_type=jnp.float32)
    spectra = spectra.reshape(2, bin_count, window_count, channel_count)
    power_bins = spectra[0] * spectra[0] + spectra[1] * spectra[1]
    same_band = (bands[:, None] == bands[None, :]).astype(jnp.float32)
    band_matrix = same_band / jnp.sum(same_band, axis=1, keepdims=True)
    band_mean = jnp.einsum("fg,gwc->fwc", band_matrix, power_bins, precision=lax.Precision.HIGHEST)
    whiten_scale = lax.rsqrt(jnp.maximum(band_mean, floor_power))
    return (spectra * whiten_scale[None]).astype(jnp.bfloat16)


def whiten_block(block, sel, count, ram, ram_count, table, band):
    halo = (block.shape[0] - sel.shape[0]) // 2
    channels = sel.shape[0]
    bins = band.shape[0]
    block = jnp.swapaxes(block.astype(jnp.float32), 0, 1)
    rows = []
    for w in range(block.shape[0]):
        x = block[w]
        neighbour_sum = jnp.dot(sel, x.astype(jnp.bfloat16), preferred_element_type=jnp.float32)
        balanced = (x[halo : halo + channels] - neighbour_sum / count).astype(jnp.bfloat16)
        ram_sum = jnp.dot(jnp.abs(balanced), ram, preferred_element_type=jnp.float32)
        envelope = ram_sum / ram_count + epsilon
        normalized = (balanced.astype(jnp.float32) / envelope).astype(jnp.bfloat16)
        spectra = lax.dot_general(
            table, normalized, (((1,), (1,)), ((), ())), preferred_element_type=jnp.float32
        )
        real, imag = spectra[:bins], spectra[bins:]
        power = real * real + imag * imag
        band_mean = jnp.dot(band, power, precision=lax.Precision.HIGHEST, preferred_element_type=jnp.float32)
        scale = lax.rsqrt(jnp.maximum(band_mean, floor_power))
        rows.append(jnp.concatenate([real * scale, imag * scale], axis=0))
    whitened = jnp.swapaxes(jnp.stack(rows, axis=0), 0, 1)
    return whitened.reshape(2, bins, whitened.shape[1], channels)


def prepare_kernel(ext_ref, sel_ref, count_ref, ram_ref, ram_count_ref, table_ref, band_ref, out_ref):
    consts = [r[...] for r in (sel_ref, count_ref, ram_ref, ram_count_ref, table_ref, band_ref)]
    out_ref[...] = whiten_block(ext_ref[...], *consts).astype(out_ref.dtype)


def constants(first_channel, total_channels, bands, channel_count, halo_width, samples, ram_half):
    ext_rows = channel_count + 2 * halo_width
    bin_count = samples // 2
    inner = jnp.arange(channel_count, dtype=jnp.int32)
    outer = jnp.arange(ext_rows, dtype=jnp.int32)
    offset = outer[None, :] - inner[:, None]
    outer_position = first_channel - halo_width + outer
    inside = (outer_position >= 0) & (outer_position < total_channels)
    selector = (offset >= 0) & (offset <= 2 * halo_width) & inside[None, :]
    neighbour_count = jnp.sum(selector.astype(jnp.float32), axis=1)[:, None]
    sample_index = np.arange(samples, dtype=np.int32)
    ram_band = np.abs(sample_index[:, None] - sample_index[None, :]) <= ram_half
    ram_count = np.sum(ram_band.astype(np.float32), axis=0)[None, :]
    frequency = np.arange(1, bin_count + 1, dtype=np.int32)
    phase_steps = frequency[:, None] * sample_index[None, :] % samples
    phase = np.float32(2.0 * math.pi / samples) * phase_steps.astype(np.float32)
    dft_table = jnp.asarray(
        (np.concatenate([np.cos(phase), -np.sin(phase)], axis=0) / np.float32(math.sqrt(samples))).astype(
            ml_dtypes.bfloat16
        )
    )
    ram_count = jnp.asarray(ram_count)
    ram_band = jnp.asarray(ram_band)
    same_band = (bands[:, None] == bands[None, :]).astype(jnp.float32)
    band_matrix = same_band / jnp.sum(same_band, axis=1, keepdims=True)
    return [
        selector.astype(jnp.bfloat16),
        neighbour_count,
        ram_band.astype(jnp.bfloat16),
        ram_count,
        dft_table,
        band_matrix,
    ]


def prepare_fast(extended, consts, windows, step=16):
    ext_rows, _, samples = extended.shape
    channel_count = consts[0].shape[0]
    bin_count = samples // 2
    whole = lambda i: (0, 0)
    return pl.pallas_call(
        prepare_kernel,
        out_shape=jax.ShapeDtypeStruct((2, bin_count, windows, channel_count), jnp.bfloat16),
        grid=(windows // step,),
        in_specs=[pl.BlockSpec((ext_rows, step, samples), lambda i: (0, i, 0))]
        + [pl.BlockSpec(c.shape, whole) for c in consts],
        out_specs=pl.BlockSpec((2, bin_count, step, channel_count), lambda i: (0, 0, i, 0)),
    )(extended, *consts)


def correlate_chunk(own, partner, acc, out, r, rows, scale, mode):
    dims = (((0,), (0,)), ((), ()))
    width = own.shape[-1]
    real_rows, imag_rows = [], []
    for j in range(rows.size):
        f = rows.start + j
        x = own[:, f]
        y = partner[:, f]
        lhs = x.reshape(-1, x.shape[-1])
        real_rhs = y.reshape(-1, y.shape[-1])
        imag_rhs = jnp.concatenate([-y[1], y[0]], axis=0)
        rhs = jnp.concatenate([real_rhs, imag_rhs], axis=1)
        both = lax.dot_general(lhs, rhs, dims, preferred_element_type=jnp.float32)
        if mode == "first":
            acc[r, f] = both
        elif mode == "middle":
            acc[r, f] = acc[r, f] + both
        else:
            total = acc[r, f] + both
            real_rows.append(total[:, :width] / scale)
            imag_rows.append(total[:, width:] / scale)
    if mode == "last":
        out[:, r, 0, rows, :] = jnp.stack(real_rows, axis=1).astype(out.dtype)
        out[:, r, 1, rows, :] = jnp.stack(imag_rows, axis=1).astype(out.dtype)


def exchange_kernel(n, chunks, scale, step, bounds, traces, ram, ram_count, table, band,
                    out, head, tail, owns, first, second, acc, halo_send, halo_recv,
                    first_send, first_recv, second_send, second_recv):
    me = lax.axis_index("blk")
    core = lax.rem(me, 2)
    down = lax.rem(me + n - 2, n)
    up = lax.rem(me + 2, n)
    left = lax.rem(me + n - 1, n)
    right = lax.rem(me + 1, n)
    mate = me + 1 - 2 * core
    halo = head.shape[0]
    channels = traces.shape[0]

    barrier = pltpu.get_barrier_semaphore()
    for peer in (down, up, left, right):
        pl.semaphore_signal(barrier, inc=1, device_id=(peer,), device_id_type=MESH)
    pl.semaphore_wait(barrier, 4)

    to_right = pltpu.make_async_remote_copy(
        traces.at[pl.ds(channels - halo, halo)], head, halo_send.at[0], halo_recv.at[0],
        device_id=(right,), device_id_type=MESH)
    to_left = pltpu.make_async_remote_copy(
        traces.at[pl.ds(0, halo)], tail, halo_send.at[1], halo_recv.at[1],
        device_id=(left,), device_id_type=MESH)
    to_right.start()
    to_left.start()

    size = owns[0].shape[1] // chunks

    def part(i):
        return pl.ds(pl.multiple_of(i * size, size), size)

    def to_down(p, i):
        return pltpu.make_async_remote_copy(
            owns[p].at[:, part(i)], second[p].at[:, part(i)], second_send.at[p, i], second_recv.at[p, i],
            device_id=(down,), device_id_type=MESH)

    def to_mate(src, p, i):
        return pltpu.make_async_remote_copy(
            src.at[:, part(i)], first[p].at[:, part(i)], first_send.at[p, i], first_recv.at[p, i],
            device_id=(mate,), device_id_type=MESH)

    def send_part(p):
        @pl.loop(0, chunks)
        def _(i):
            to_down(p, i).start()

        @pl.when(core == 1)
        def _():
            @pl.loop(0, chunks)
            def _(i):
                to_mate(owns[p], p, i).start()

    shape = (channels, channels + 2 * halo)
    offset = lax.broadcasted_iota(jnp.int32, shape, 1) - lax.broadcasted_iota(jnp.int32, shape, 0)
    position = me * channels - halo + lax.broadcasted_iota(jnp.int32, shape, 1)
    inside = (position >= 0) & (position < n * channels)
    selector = ((offset >= 0) & (offset <= 2 * halo) & inside).astype(jnp.float32)
    count = jnp.sum(selector, axis=1, keepdims=True)
    consts = [selector.astype(jnp.bfloat16), count] + [r[...] for r in (ram, ram_count, table, band)]
    to_right.wait_recv()
    to_left.wait_recv()
    for p, (start, length) in enumerate(bounds):
        late = owns[p]

        @pl.loop(0, length // step)
        def _(b):
            src = pl.ds(pl.multiple_of(start + b * step, step), step)
            dst = pl.ds(pl.multiple_of(b * step, step), step)
            block = jnp.concatenate([head[:, src, :], traces[:, src, :], tail[:, src, :]], axis=0)
            late[:, :, dst, :] = whiten_block(block, *consts).astype(late.dtype)

        send_part(p)

    parts = len(owns)
    for p in range(parts):
        mode = "first" if p == 0 else ("last" if p == parts - 1 else "middle")

        @pl.loop(0, chunks)
        def _(i):
            to_down(p, i).wait_recv()

            @pl.when(core == 0)
            def _():
                to_mate(second[p], p, i).start()

            correlate_chunk(owns[p], second[p], acc, out, 1, part(i), scale, mode)
            to_mate(second[p], p, i).wait_recv()
            correlate_chunk(owns[p], first[p], acc, out, 0, part(i), scale, mode)

    to_right.wait_send()
    to_left.wait_send()

    @pl.loop(0, chunks)
    def _(i):
        for p in range(parts):
            to_down(p, i).wait_send()
            to_mate(second[p], p, i).wait_send()


def per_device(traces, bands, chunks=4, split=(16, 32, 48, 48), step=16):
    channel_count, window_count, samples = traces.shape
    n = lax.axis_size("blk")
    first_channel = lax.axis_index("blk") * channel_count
    consts = constants(first_channel, channel_count * n, bands, channel_count, HW, samples, RAM_HALF)
    bounds, start = [], 0
    for length in split:
        bounds.append((start, length))
        start += length
    bins = samples // 2
    shapes = [(2, bins, length, channel_count) for length in split]
    buffers = lambda: [pltpu.VMEM(shape, jnp.bfloat16) for shape in shapes]
    vmem = pl.BlockSpec(memory_space=pltpu.VMEM)
    parts = len(split)
    return pl.pallas_call(
        functools.partial(exchange_kernel, n, chunks, math.sqrt(window_count), step, bounds),
        out_shape=jax.ShapeDtypeStruct((channel_count, ROUNDS, 2, bins, channel_count), jnp.bfloat16),
        in_specs=[vmem] * 5,
        out_specs=vmem,
        scratch_shapes=[
            pltpu.VMEM((HW, window_count, samples), jnp.bfloat16),
            pltpu.VMEM((HW, window_count, samples), jnp.bfloat16),
            buffers(),
            buffers(),
            buffers(),
            pltpu.VMEM((ROUNDS, bins, channel_count, 2 * channel_count), jnp.float32),
            pltpu.SemaphoreType.DMA((2,)),
            pltpu.SemaphoreType.DMA((2,)),
            pltpu.SemaphoreType.DMA((parts, chunks)),
            pltpu.SemaphoreType.DMA((parts, chunks)),
            pltpu.SemaphoreType.DMA((parts, chunks)),
            pltpu.SemaphoreType.DMA((parts, chunks)),
        ],
        compiler_params=pltpu.CompilerParams(
            collective_id=0, has_side_effects=True, vmem_limit_bytes=63 * 1024 * 1024
        ),
    )(traces, *consts[2:])


def solution(mesh):
    placed = (P("blk", None, None), P())
    return jax.shard_map(
        per_device,
        mesh=mesh,
        in_specs=placed,
        out_specs=P("blk", None, None, None, None),
        check_vma=False,
    )
```
